32 devices in a mesh: radial: 1, mode: 32 (over z, y, x, core).
Axes of the slice: x: 2, y: 2, z: 4, core: 2. Of those that a mesh axis runs over, the one named last changes fastest.
Arguments:
- spectral_state: float32 [64, 3, 2, 2, 129], P('mode', None, 'radial'), may hold values from -6 to 6
- synthesis_table: bfloat16 [64, 129, 128], P('mode', None, 'radial'), may hold values from -0.03125 to 0.03125
- low_orders: int32 [64], replicated, may hold values from 0 to 63, each once
- diffusion: float32 [3], replicated, may hold values from 200 to 2000
- coupling: float32 [3], replicated, may hold values from 1 to 4
Outputs:
- updated: float32 [64, 3, 2, 2, 129], P('mode', None, 'radial')
The draws below stay inside these ranges and needn't reach their ends.
Inputs may be any that keep to these rules, and one draw needn't show every extreme that they name: A permutation: pair j holds the orders low_orders[j] and 127 - low_orders[j].
All inputs are finite; a program needn't handle non-finite values.
Results may differ from the reference program's by a relative error of at most 0.0023.
The reference program's roundings to bfloat16 on the way (of `legendre`, `coeffs`, `fourier` and `returned`) count: a program that leaves them out, or rounds other values in their place, can miss the bound.
Values may be sent and summed in bfloat16 or wider, within the bound.
No kernel may reach another device: no remote copies, remote signals or barrier semaphores. Data moves between devices by JAX's collectives and lax.ppermute only.
A program may use at most 64 MiB of HBM per device.

```python
import math
import jax
import jax.numpy as jnp
from jax import lax

ORDERS = 128
PAIRS = 64
ROWS = 129
NLAT = 256
NH = 128
NLON = 384
SHELLS = 2


def level_of(stream_key, shape, cuts, smallest, top_value):
    def one(axis_at, parts):
        heights = jax.random.uniform(jax.random.fold_in(jax.random.fold_in(stream_key, 6), axis_at), (parts,), jnp.float32, smallest / len(cuts), top_value / len(cuts))
        return jnp.repeat(jnp.exp(heights), shape[axis_at] // parts).reshape((-1,) + (1,) * (len(shape) - axis_at - 1))

    gain = one(*cuts[0])
    for cut in cuts[1:]:
        gain = gain * one(*cut)
    return gain


def scatter_about(own_key, extent, scale, bound, shards=(), kind=jnp.bfloat16):
    loudness = level_of(own_key, extent, shards, -0.22, 0.18) if shards else 1.0
    entries = jax.random.normal(own_key, extent, jnp.float32) * scale * loudness
    return jnp.minimum(jnp.maximum(entries, -bound), bound).astype(kind)


def setup_inputs(seed: int = 0) -> dict:
    splits = jax.random.split(jax.random.key(seed), 6)
    return {
        "spectral_state": scatter_about(splits[0], (PAIRS, 3, SHELLS, 2, ROWS), 1.0, 6.0, ((0, 32),), jnp.float32),
        "synthesis_table": scatter_about(splits[1], (PAIRS, ROWS, NH), (2 * ORDERS * ROWS) ** -0.5, 0.03125, ((0, 32),)),
        "low_orders": jax.random.permutation(splits[2], PAIRS).astype(jnp.int32),
        "diffusion": jnp.clip(jnp.exp(jax.random.uniform(splits[3], (3,), jnp.float32, math.log(200.0), math.log(2000.0))), 200.0, 2000.0),
        "coupling": jnp.clip(jax.random.uniform(splits[4], (3,), jnp.float32, 1.0, 4.0), 1.0, 4.0),
    }


inner_radius = 0.538
shell_step = 1.0 / 2048.0

def pair_layout(low_orders):
    row_index = jnp.arange(ORDERS + 1, dtype=jnp.int32)[None, :]
    lower_col = low_orders.astype(jnp.int32)[:, None]
    in_lower = row_index < ORDERS - lower_col
    degree = jnp.where(in_lower, lower_col + row_index, row_index - 1)
    order_of = jnp.where(in_lower, lower_col, ORDERS - 1 - lower_col)
    return (in_lower, degree, order_of)

def full_table(pair_table, pair_sign):
    northern = pair_table.astype(jnp.float32)
    southern = (northern * pair_sign[:, None])[:, ::-1]
    return jnp.concatenate([northern, southern], axis=1)

def reference(spectral_state, synthesis_table, low_orders, diffusion, coupling):
    in_lower, degree, order_of = pair_layout(low_orders)
    row_sign = jnp.where((degree + order_of) % 2 == 0, 1.0, -1.0).astype(jnp.float32)
    order_mask = jnp.stack([in_lower, jnp.logical_not(in_lower)], axis=1).astype(jnp.float32)
    coeffs = spectral_state.astype(jnp.bfloat16)

    def synth_pair(inputs):
        pair_table, pair_sign, pair_mask, pair_coeffs = inputs
        legendre = full_table(pair_table, pair_sign)
        values = jnp.einsum('rj,fscr,kr->kfscj', legendre, pair_coeffs.astype(jnp.float32), pair_mask, precision=lax.Precision.HIGHEST)
        return values.astype(jnp.bfloat16)
    fourier = lax.map(synth_pair, (synthesis_table, row_sign, order_mask, coeffs))
    by_shell = jnp.transpose(fourier, (3, 2, 5, 0, 1, 4)).astype(jnp.float32)
    lower_orders = low_orders.astype(jnp.int32)
    flat_orders = jnp.stack([lower_orders, ORDERS - 1 - lower_orders], axis=1).reshape(ORDERS)
    analysis_scale = 2.0 * math.sqrt(ORDERS * (ORDERS + 1) / (NLAT * NLON))

    def transform_shell(values):
        values = values.reshape(3, NLAT, ORDERS, 2)
        real_part = jnp.zeros((3, NLAT, ORDERS + 1), jnp.float32).at[:, :, flat_orders].set(values[..., 0])
        imag_part = jnp.zeros((3, NLAT, ORDERS + 1), jnp.float32).at[:, :, flat_orders].set(values[..., 1])
        grid_values = NLON * jnp.fft.irfft(lax.complex(real_part, imag_part), n=NLON, axis=-1)
        products = jnp.stack([grid_values[0] * grid_values[1], grid_values[0] * grid_values[2], grid_values[1] * grid_values[2]])
        spectrum = jnp.fft.rfft(products, axis=-1)[:, :, flat_orders]
        result = jnp.stack([jnp.real(spectrum), jnp.imag(spectrum)], axis=-1) * analysis_scale
        return result.reshape(3, NLAT, PAIRS, 2, 2).astype(jnp.bfloat16)
    returned = lax.map(transform_shell, by_shell)
    returned = jnp.transpose(returned, (3, 4, 1, 0, 5, 2))

    def analyse_pair(inputs):
        pair_table, pair_sign, pair_mask, pair_back = inputs
        legendre = full_table(pair_table, pair_sign)
        return jnp.einsum('rj,kfscj,kr->fscr', legendre, pair_back.astype(jnp.float32), pair_mask, precision=lax.Precision.HIGHEST)
    nonlinear = lax.map(analyse_pair, (synthesis_table, row_sign, order_mask, returned))
    degree_term = degree.astype(jnp.float32)
    radius = inner_radius + (jnp.arange(SHELLS, dtype=jnp.float32) + 0.5) * shell_step
    damping = (degree_term * (degree_term + 1.0))[:, None, None, None, :] * (shell_step * shell_step) / (radius * radius)[None, None, :, None, None]
    rate_full = diffusion.reshape(1, 3, 1, 1, 1)
    strength = coupling.reshape(1, 3, 1, 1, 1)
    padded = jnp.pad(spectral_state, ((0, 0), (0, 0), (1, 1), (0, 0), (0, 0)))
    laplace = padded[:, :, 2:] - 2.0 * spectral_state + padded[:, :, :-2] - damping * spectral_state
    drive = spectral_state + rate_full * (laplace + strength * nonlinear)
    diagonal = jnp.broadcast_to(1.0 + rate_full * (2.0 + damping), drive.shape)
    drive_by = jnp.moveaxis(drive, 2, 0)
    diagonal_by = jnp.moveaxis(diagonal, 2, 0)
    rate_col = diffusion.reshape(1, 3, 1, 1)
    blank_state = jnp.zeros(drive_by.shape[1:], jnp.float32)

    def forward(running, inputs):
        pivot, solved = running
        diag_now, drive_now = inputs
        denom_now = diag_now + rate_col * pivot
        pivot_new = -rate_col / denom_now
        solved_new = (drive_now + rate_col * solved) / denom_now
        return ((pivot_new, solved_new), (pivot_new, solved_new))
    _, (pivots, solveds) = lax.scan(forward, (blank_state, blank_state), (diagonal_by, drive_by))

    def backward(next_value, inputs):
        pivot, solved = inputs
        value = solved - pivot * next_value
        return (value, value)
    _, updated_by = lax.scan(backward, blank_state, (pivots, solveds), reverse=True)
    return jnp.moveaxis(updated_by, 0, 2)
```

```python
import functools
import math

import jax
import jax.numpy as jnp
from jax import lax
from jax.experimental import pallas as pl
from jax.experimental.pallas import tpu as pltpu
from jax.sharding import PartitionSpec as P

inner_radius = 0.538
shell_step = 1.0 / 2048.0
LANES = 128
GRANT = pltpu.CompilerParams(vmem_limit_bytes=16 * 1024 * 1024)
NT = (((1,), (1,)), ((), ()))


def with_halo(shard, axis, dim, width):
    count, length = (lax.axis_size(axis), shard.shape[dim])
    up = [(i, (i + 1) % count) for i in range(count - 1)]
    down = [(j, i) for i, j in up]
    last = lax.slice_in_dim(shard, length - width, length, axis=dim)
    first = lax.slice_in_dim(shard, 0, width, axis=dim)
    before = lax.ppermute(last, axis, up)
    after = lax.ppermute(first, axis, down)
    return jnp.concatenate([before, shard, after], axis=dim)


def row_factors(lower, shape, orders_total):
    row = lax.broadcasted_iota(jnp.int32, shape, len(shape) - 1)
    in_lower = row < orders_total - lower
    odd_lower = lax.rem(row, 2) == 1
    odd_upper = lax.rem(row + orders_total - lower, 2) == 1
    members = (in_lower, jnp.logical_not(in_lower))
    signs = (jnp.where(odd_lower, -1.0, 1.0), jnp.where(odd_upper, -1.0, 1.0))
    return members, signs


def state_rows(state_ref, pair, part, fields):
    shells = state_ref.shape[2]
    rows = [state_ref[pair, f, s, part : part + 1, :] for f in fields for s in range(shells)]
    return jnp.concatenate(rows, axis=0)


def fill_waves(low_row, orders_total, high_ref, rest_ref, step):
    columns, lon_total = high_ref.shape
    width = lon_total // 3
    lon = lax.broadcasted_iota(jnp.int32, (step, width), 1).astype(jnp.float32)
    pair_lane = lax.broadcasted_iota(jnp.int32, (step, low_row.shape[1]), 1)
    third = math.sqrt(0.75)

    def fill(base):
        column = base + lax.broadcasted_iota(jnp.int32, (step, 1), 0)
        hit = pair_lane == column // 4
        lower = jnp.sum(jnp.where(hit, low_row, 0.0), axis=1, keepdims=True)
        is_lower = (column // 2) % 2 == 0
        is_cosine = column % 2 == 0
        order = jnp.where(is_lower, lower, orders_total - 1 - lower)
        turns = order * lon
        quad = jnp.floor(turns * (4.0 / lon_total) + 0.5)
        angle = (turns - quad * (lon_total / 4)) * (2.0 * math.pi / lon_total)
        square = angle * angle
        cosine = 1.0 + square * (
            -0.5 + square * (1.0 / 24 + square * (-1.0 / 720 + square * (1.0 / 40320)))
        )
        sine = 1.0 / 120 + square * (-1.0 / 5040 + square * (1.0 / 362880))
        sine = angle * (1.0 + square * (-1.0 / 6 + square * sine))
        quad = quad.astype(jnp.int32)
        swap = (quad & 1) == 1
        cosine, sine = (jnp.where(swap, sine, cosine), jnp.where(swap, cosine, sine))
        cosine = jnp.where(((quad + 1) & 2) == 2, -cosine, cosine)
        sine = jnp.where((quad & 2) == 2, -sine, sine)
        for at in range(3):
            turn = at * order
            turn = turn - 3.0 * jnp.floor((turn + 0.5) * (1.0 / 3.0))
            cos_at = jnp.where(turn == 0.0, 1.0, -0.5)
            sin_at = jnp.where(turn == 0.0, 0.0, jnp.where(turn == 1.0, third, -third))
            by_cosine = jnp.where(is_cosine, cos_at, -sin_at)
            by_sine = jnp.where(is_cosine, -sin_at, -cos_at)
            value = cosine * by_cosine + sine * by_sine
            high = value.astype(jnp.bfloat16)
            high_ref[pl.ds(base, step), at * width : (at + 1) * width] = high
            rest_ref[pl.ds(base, step), at * width : (at + 1) * width] = (
                value - high.astype(jnp.float32)
            ).astype(jnp.bfloat16)

    if columns <= 256:
        for base in range(0, columns, step):
            fill(base)
    else:

        @pl.loop(0, columns // step)
        def _(at):
            fill(pl.multiple_of(at * step, step))


def synthesis_kernel(
    dims, low_ref, low_row_ref, state_ref, table_ref, out_ref, high_ref, rest_ref, spread_ref
):
    pairs_dev, block, mode_count, orders_total = dims
    fields = state_ref.shape[1]
    rows_total = state_ref.shape[-1]
    chunk_rows = out_ref.shape[0] // mode_count
    group = lax.axis_index("mode") * pairs_dev
    pieces = []
    for pair in range(pairs_dev):
        lower = low_ref[group + pair]
        members, signs = row_factors(lower, (1, rows_total), orders_total)
        coeffs = [state_rows(state_ref, pair, part, (*range(fields), 0)) for part in range(2)]
        left = []
        for k in range(2):
            order = lower if k == 0 else orders_total - 1 - lower
            weight = jnp.where(order == 0, 1.0, 2.0)
            member = jnp.where(members[k], weight, 0.0)
            for part in range(2):
                left.append(coeffs[part] * member)
                left.append(coeffs[part] * (member * signs[k]))
        left = jnp.concatenate(left, axis=0).astype(jnp.bfloat16)
        pieces.append(jnp.dot(left, table_ref[pair], preferred_element_type=jnp.float32))
    fourier = jnp.concatenate(pieces, axis=0).astype(jnp.bfloat16).astype(jnp.float32)
    turned = fourier.T
    lane_block = lax.broadcasted_iota(jnp.int32, (mode_count, LANES), 1) // block
    count = turned.shape[0] // mode_count
    for row in range(chunk_rows):
        merged = jnp.zeros((mode_count, LANES), jnp.float32)
        for i in range(count):
            part = turned[i * mode_count : (i + 1) * mode_count]
            moved = pltpu.roll(part, (block * (i - row)) % LANES, 1)
            merged = jnp.where(lane_block == i, moved, merged)
        spread_ref[:, row, :] = merged
    out_ref[...] = spread_ref[...].reshape(out_ref.shape).astype(jnp.bfloat16)
    fill_waves(low_row_ref[...].astype(jnp.float32), orders_total, high_ref, rest_ref, 32)


def product_kernel(dims, sent_ref, high_ref, rest_ref, out_ref):
    used, shells, scale = dims
    turned = sent_ref[...].astype(jnp.float32).T[:used].astype(jnp.bfloat16)
    grid = jnp.dot(turned, high_ref[...], preferred_element_type=jnp.float32)
    grid = grid + jnp.dot(turned, rest_ref[...], preferred_element_type=jnp.float32)
    products = grid * pltpu.roll(grid, used - shells, 0)
    high = products.astype(jnp.bfloat16)
    rest = (products - high.astype(jnp.float32)).astype(jnp.bfloat16)
    both = lax.dot_general(
        high_ref[...], jnp.concatenate([high, rest], axis=0), NT, preferred_element_type=jnp.float32
    )
    totals = lax.dot_general(rest_ref[...], high, NT, preferred_element_type=jnp.float32)
    totals = totals + both[:, :used] + both[:, used:]
    answers = (totals * scale).astype(jnp.bfloat16)
    out_ref[...] = jnp.concatenate(
        [answers, jnp.zeros((answers.shape[0], LANES - used), jnp.bfloat16)], axis=1
    )


def analysis_sums(dims, low_ref, sent_ref, table_ref, spread_ref, emit):
    pairs_dev, block, count, mode_count, orders_total = dims
    rows_total = table_ref.shape[1]
    chunk_rows = sent_ref.shape[0] // mode_count
    group = lax.axis_index("mode") * pairs_dev
    spread_ref[...] = sent_ref[...].astype(jnp.float32).reshape(spread_ref.shape)
    lane_block = lax.broadcasted_iota(jnp.int32, (mode_count, LANES), 1) // block
    parts = [jnp.zeros((mode_count, LANES), jnp.float32) for _ in range(count)]
    for row in range(chunk_rows):
        piece = spread_ref[:, row, :]
        for i in range(count):
            moved = pltpu.roll(piece, (block * (row - i)) % LANES, 1)
            parts[i] = jnp.where(lane_block == row, moved, parts[i])
    returned = jnp.concatenate(parts, axis=0).T.astype(jnp.bfloat16)
    per_pair = returned.shape[0] // pairs_dev
    half = block // 2
    for pair in range(pairs_dev):
        lower = low_ref[group + pair]
        members, signs = row_factors(lower, (1, rows_total), orders_total)
        sums = lax.dot_general(
            returned[pair * per_pair : (pair + 1) * per_pair],
            table_ref[pair],
            NT,
            preferred_element_type=jnp.float32,
        )
        for part in range(2):
            total = jnp.zeros((half, rows_total), jnp.float32)
            for k in range(2):
                at = (k * 2 + part) * block
                north = sums[at : at + half]
                south = sums[at + half : at + block]
                total = jnp.where(members[k], north + signs[k] * south, total)
            emit(pair, part, lower, total)


def analysis_kernel(dims, low_ref, sent_ref, table_ref, out_ref, spread_ref):
    def emit(pair, part, lower, total):
        out_ref[pair, part] = total

    analysis_sums(dims, low_ref, sent_ref, table_ref, spread_ref, emit)


def step_kernel(
    dims, low_ref, rate_ref, coupling_ref, sent_ref, table_ref, state_ref, out_ref, spread_ref
):
    orders_total = dims[-1]
    rows_total = table_ref.shape[1]
    half = dims[1] // 2
    fields = (0, 2, 1, 0)
    at = lax.broadcasted_iota(jnp.int32, (half, 1), 0)
    upper = at % 2 == 1
    by_field = [at // 2 == 1, at // 2 == 2]

    def column(ref):
        first = jnp.full((half, 1), ref[0], jnp.float32)
        return jnp.where(by_field[0], ref[2], jnp.where(by_field[1], ref[1], first))

    def other(value):
        return jnp.where(upper, pltpu.roll(value, 1, 0), pltpu.roll(value, half - 1, 0))

    rate = column(rate_ref)
    strength = column(coupling_ref)
    radius = inner_radius + (jnp.where(upper, 1.0, 0.0) + 0.5) * shell_step
    inverse = (shell_step * shell_step) / (radius * radius)
    row = lax.broadcasted_iota(jnp.int32, (1, rows_total), 1)
    cache = {}

    def emit(pair, part, lower, total):
        if pair not in cache:
            degree = jnp.where(row < orders_total - lower, lower + row, row - 1).astype(jnp.float32)
            damping = (degree * (degree + 1.0)) * inverse
            diagonal = 1.0 + rate * (2.0 + damping)
            crossed = other(diagonal)
            factor = 1.0 / (diagonal * crossed - rate * rate)
            cache[pair] = (damping, crossed * factor, rate * factor)
        damping, own, across = cache[pair]
        state = state_rows(state_ref, pair, part, fields)
        laplace = other(state) - 2.0 * state - damping * state
        drive = state + rate * (laplace + strength * total)
        updated = own * drive + across * other(drive)
        for k, f in enumerate(fields[:3]):
            for s in range(2):
                out_ref[pair, f, s, part : part + 1, :] = updated[2 * k + s : 2 * k + s + 1]

    analysis_sums(dims, low_ref, sent_ref, table_ref, spread_ref, emit)


def vmem(count):
    return [pl.BlockSpec(memory_space=pltpu.VMEM)] * count


def body(spectral_state, synthesis_table, low_orders, diffusion, coupling):
    radial_count = lax.axis_size("radial")
    if radial_count > 1:
        synthesis_table = lax.all_gather(synthesis_table, "radial", axis=2, tiled=True)
    pairs_dev, field_count, shell_count, part_count, rows_total = spectral_state.shape
    half_lat = synthesis_table.shape[2]
    lat_total = 2 * half_lat
    orders_total = rows_total - 1
    lon_total = 3 * orders_total
    mode_count = lax.axis_size("mode")
    chunk_rows = pairs_dev * 2 * part_count
    column_count = chunk_rows * mode_count
    count = half_lat // mode_count
    half = (field_count + 1) * shell_count
    block = 2 * half
    used = count * block
    assert half == 8 and chunk_rows * block == LANES and used <= LANES // 2 and part_count == 2
    scale = 2.0 * math.sqrt(orders_total * rows_total / (lat_total * lon_total))
    low_orders = low_orders.astype(jnp.int32)
    smem = pl.BlockSpec(memory_space=pltpu.SMEM)
    spread = pltpu.VMEM((mode_count, chunk_rows, LANES), jnp.float32)
    sent = jax.ShapeDtypeStruct((column_count, LANES), jnp.bfloat16)
    table_shape = jax.ShapeDtypeStruct((column_count, lon_total), jnp.bfloat16)
    chunks, wave_high, wave_rest = pl.pallas_call(
        functools.partial(synthesis_kernel, (pairs_dev, block, mode_count, orders_total)),
        out_shape=[sent, table_shape, table_shape],
        in_specs=[smem] + vmem(3),
        out_specs=vmem(3),
        scratch_shapes=[spread],
        compiler_params=GRANT,
        name="synthesis",
    )(low_orders, low_orders[None, :], spectral_state, synthesis_table)
    pieces = lax.all_to_all(chunks, "mode", split_axis=0, concat_axis=0, tiled=True)
    answers = pl.pallas_call(
        functools.partial(product_kernel, (used, shell_count, scale)),
        out_shape=sent,
        in_specs=vmem(3),
        out_specs=pl.BlockSpec(memory_space=pltpu.VMEM),
        compiler_params=GRANT,
        name="products",
    )(pieces, wave_high, wave_rest)
    returned = lax.all_to_all(answers, "mode", split_axis=0, concat_axis=0, tiled=True)
    dims = (pairs_dev, block, count, mode_count, orders_total)
    if radial_count == 1 and shell_count == 2:
        return pl.pallas_call(
            functools.partial(step_kernel, dims),
            out_shape=jax.ShapeDtypeStruct(spectral_state.shape, jnp.float32),
            in_specs=[smem] * 3 + vmem(3),
            out_specs=pl.BlockSpec(memory_space=pltpu.VMEM),
            scratch_shapes=[spread],
            compiler_params=GRANT,
            name="step",
        )(low_orders, diffusion, coupling, returned, synthesis_table, spectral_state)
    nonlinear = pl.pallas_call(
        functools.partial(analysis_kernel, dims),
        out_shape=jax.ShapeDtypeStruct((pairs_dev, part_count, half, rows_total), jnp.float32),
        in_specs=[smem] + vmem(2),
        out_specs=pl.BlockSpec(memory_space=pltpu.VMEM),
        scratch_shapes=[spread],
        compiler_params=GRANT,
        name="analysis",
    )(low_orders, returned, synthesis_table)
    nonlinear = nonlinear.reshape(pairs_dev, part_count, field_count + 1, shell_count, rows_total)
    nonlinear = jnp.stack([nonlinear[:, :, 0], nonlinear[:, :, 2], nonlinear[:, :, 1]], axis=1)
    nonlinear = nonlinear.transpose(0, 1, 3, 2, 4)
    return solve(spectral_state, nonlinear, low_orders, diffusion, coupling)


def solve(spectral_state, nonlinear, low_orders, diffusion, coupling):
    pairs_dev, field_count, shell_count, part_count, rows_total = spectral_state.shape
    orders_total = rows_total - 1
    radial_count = lax.axis_size("radial")
    own = lax.dynamic_slice_in_dim(low_orders, lax.axis_index("mode") * pairs_dev, pairs_dev)
    row_index = lax.iota(jnp.int32, rows_total)[None, :]
    lower_col = own[:, None]
    degree = jnp.where(row_index < orders_total - lower_col, lower_col + row_index, row_index - 1)
    radial_at = lax.axis_index("radial")
    rate_col = diffusion.reshape(1, field_count, 1, 1)
    strength = coupling.reshape(1, field_count, 1, 1)
    degree_term = degree.astype(jnp.float32)
    degree_term = (degree_term * (degree_term + 1.0))[:, None, None, :] * (shell_step * shell_step)
    if radial_count > 1:
        with_edges = with_halo(spectral_state, "radial", 2, 1)
    else:
        with_edges = jnp.pad(spectral_state, ((0, 0), (0, 0), (1, 1), (0, 0), (0, 0)))
    diagonals = []
    drives = []
    for shell_at in range(shell_count):
        radius = (
            inner_radius
            + ((radial_at * shell_count + shell_at).astype(jnp.float32) + 0.5) * shell_step
        )
        damping = degree_term / (radius * radius)
        middle = with_edges[:, :, shell_at + 1]
        laplace = (
            with_edges[:, :, shell_at + 2]
            - 2.0 * middle
            + with_edges[:, :, shell_at]
            - damping * middle
        )
        drives.append(middle + rate_col * (laplace + strength * nonlinear[:, :, shell_at]))
        diagonals.append(1.0 + rate_col * (2.0 + damping))
    narrow_zero = jnp.zeros(diagonals[0].shape, jnp.float32)
    wide_zero = jnp.zeros(drives[0].shape, jnp.float32)
    pivot_prev = narrow_zero
    carry_u, carry_v, carry_w = (wide_zero, narrow_zero, narrow_zero)
    pivots, sweep_u, sweep_v, sweep_w = ([], [], [], [])
    for shell_at in range(shell_count):
        denom_at = diagonals[shell_at] + rate_col * pivot_prev
        pivot_prev = -rate_col / denom_at
        first_drive = rate_col if shell_at == 0 else 0.0
        last_drive = rate_col if shell_at == shell_count - 1 else 0.0
        carry_u = (drives[shell_at] + rate_col * carry_u) / denom_at
        carry_v = (first_drive + rate_col * carry_v) / denom_at
        carry_w = (last_drive + rate_col * carry_w) / denom_at
        pivots.append(pivot_prev)
        sweep_u.append(carry_u)
        sweep_v.append(carry_v)
        sweep_w.append(carry_w)
    solved_u, solved_v, solved_w = ([sweep_u[-1]], [sweep_v[-1]], [sweep_w[-1]])
    for shell_at in range(shell_count - 2, -1, -1):
        solved_u.insert(0, sweep_u[shell_at] - pivots[shell_at] * solved_u[0])
        solved_v.insert(0, sweep_v[shell_at] - pivots[shell_at] * solved_v[0])
        solved_w.insert(0, sweep_w[shell_at] - pivots[shell_at] * solved_w[0])
    if radial_count == 1:
        return jnp.stack(solved_u, axis=2)
    first_u, last_u = (solved_u[0], solved_u[-1])
    first_v, last_v = (solved_v[0], solved_v[-1])
    first_w, last_w = (solved_w[0], solved_w[-1])
    wide_rows = jnp.stack([first_u, last_u])[None]
    narrow_rows = jnp.stack([first_v, first_w, last_v, last_w])[None]
    wide_all, narrow_all = (
        lax.all_gather(wide_rows, "radial", axis=0, tiled=True),
        lax.all_gather(narrow_rows, "radial", axis=0, tiled=True),
    )
    chain_count = lax.axis_size("radial")
    alpha_now, beta_now = (wide_zero, narrow_zero)
    alphas, betas = ([], [])
    for member in range(chain_count):
        alphas.append(alpha_now)
        betas.append(beta_now)
        peer_first_u, peer_last_u = (wide_all[member, 0], wide_all[member, 1])
        peer_first_v, peer_first_w = (narrow_all[member, 0], narrow_all[member, 1])
        peer_last_v, peer_last_w = (narrow_all[member, 2], narrow_all[member, 3])
        shrink = 1.0 - peer_first_v * beta_now
        alpha_new = (
            peer_last_u
            - peer_last_u * peer_first_v * beta_now
            + peer_last_v * alpha_now
            + peer_last_v * peer_first_u * beta_now
        ) / shrink
        beta_new = (
            peer_last_w
            - peer_last_w * peer_first_v * beta_now
            + peer_last_v * peer_first_w * beta_now
        ) / shrink
        alpha_now, beta_now = (alpha_new, beta_new)
    next_first = wide_zero
    firsts = [None] * chain_count
    nexts = [None] * chain_count
    for member in range(chain_count - 1, -1, -1):
        nexts[member] = next_first
        peer_first_u = wide_all[member, 0]
        peer_first_v, peer_first_w = (narrow_all[member, 0], narrow_all[member, 1])
        next_first = (peer_first_u + peer_first_v * alphas[member] + peer_first_w * next_first) / (
            1.0 - peer_first_v * betas[member]
        )
        firsts[member] = next_first
    alpha_prev = lax.dynamic_index_in_dim(jnp.stack(alphas), radial_at, 0, keepdims=False)
    beta_prev = lax.dynamic_index_in_dim(jnp.stack(betas), radial_at, 0, keepdims=False)
    own_first = lax.dynamic_index_in_dim(jnp.stack(firsts), radial_at, 0, keepdims=False)
    next_first = lax.dynamic_index_in_dim(jnp.stack(nexts), radial_at, 0, keepdims=False)
    prev_last = alpha_prev + beta_prev * own_first
    outputs = []
    for shell_at in range(shell_count):
        outputs.append(
            solved_u[shell_at] + prev_last * solved_v[shell_at] + next_first * solved_w[shell_at]
        )
    return jnp.stack(outputs, axis=2)


def solution(mesh):
    placed = (P("mode", None, "radial", None, None), P("mode", None, "radial"), P(), P(), P())
    return jax.shard_map(
        body,
        mesh=mesh,
        in_specs=placed,
        out_specs=P("mode", None, "radial", None, None),
        check_vma=False,
    )
```

```python
import functools
import math

import jax
import jax.numpy as jnp
from jax import lax
from jax.experimental import pallas as pl
from jax.experimental.pallas import tpu as pltpu
from jax.sharding import PartitionSpec as P

inner_radius = 0.538
shell_step = 1.0 / 2048.0
LANES = 128
GRANT = pltpu.CompilerParams(vmem_limit_bytes=16 * 1024 * 1024)
NT = (((1,), (1,)), ((), ()))


def with_halo(shard, axis, dim, width):
    count, length = (lax.axis_size(axis), shard.shape[dim])
    up = [(i, (i + 1) % count) for i in range(count - 1)]
    down = [(j, i) for i, j in up]
    last = lax.slice_in_dim(shard, length - width, length, axis=dim)
    first = lax.slice_in_dim(shard, 0, width, axis=dim)
    before = lax.ppermute(last, axis, up)
    after = lax.ppermute(first, axis, down)
    return jnp.concatenate([before, shard, after], axis=dim)


def own_lower(low_ref, at):
    low_row = low_ref[...][None, :]
    lane = lax.broadcasted_iota(jnp.int32, low_row.shape, 1)
    return jnp.sum(jnp.where(lane == at, low_row, 0), axis=1, keepdims=True)


def row_factors(lower, shape, orders_total):
    row = lax.broadcasted_iota(jnp.int32, shape, len(shape) - 1)
    in_lower = row < orders_total - lower
    odd_lower = lax.rem(row, 2) == 1
    odd_upper = lax.rem(row + orders_total - lower, 2) == 1
    members = (in_lower, jnp.logical_not(in_lower))
    signs = (jnp.where(odd_lower, -1.0, 1.0), jnp.where(odd_upper, -1.0, 1.0))
    return members, signs


def state_rows(state_ref, pair, part, fields):
    shells = state_ref.shape[2]
    rows = [state_ref[pair, f, s, part : part + 1, :] for f in fields for s in range(shells)]
    return jnp.concatenate(rows, axis=0)


def fill_waves(low_row, orders_total, high_ref, rest_ref, step):
    columns, lon_total = high_ref.shape
    width = lon_total // 3
    lon = lax.broadcasted_iota(jnp.int32, (step, width), 1).astype(jnp.float32)
    pair_lane = lax.broadcasted_iota(jnp.int32, (step, low_row.shape[1]), 1)
    third = math.sqrt(0.75)

    def fill(base):
        column = base + lax.broadcasted_iota(jnp.int32, (step, 1), 0)
        hit = pair_lane == column // 4
        lower = jnp.sum(jnp.where(hit, low_row, 0.0), axis=1, keepdims=True)
        is_lower = (column // 2) % 2 == 0
        is_cosine = column % 2 == 0
        order = jnp.where(is_lower, lower, orders_total - 1 - lower)
        turns = order * lon
        quad = jnp.floor(turns * (4.0 / lon_total) + 0.5)
        angle = (turns - quad * (lon_total / 4)) * (2.0 * math.pi / lon_total)
        square = angle * angle
        cosine = 1.0 + square * (
            -0.5 + square * (1.0 / 24 + square * (-1.0 / 720 + square * (1.0 / 40320)))
        )
        sine = 1.0 / 120 + square * (-1.0 / 5040 + square * (1.0 / 362880))
        sine = angle * (1.0 + square * (-1.0 / 6 + square * sine))
        quad = quad.astype(jnp.int32)
        swap = (quad & 1) == 1
        cosine, sine = (jnp.where(swap, sine, cosine), jnp.where(swap, cosine, sine))
        cosine = jnp.where(((quad + 1) & 2) == 2, -cosine, cosine)
        sine = jnp.where((quad & 2) == 2, -sine, sine)
        for at in range(3):
            turn = at * order
            turn = turn - 3.0 * jnp.floor((turn + 0.5) * (1.0 / 3.0))
            cos_at = jnp.where(turn == 0.0, 1.0, -0.5)
            sin_at = jnp.where(turn == 0.0, 0.0, jnp.where(turn == 1.0, third, -third))
            by_cosine = jnp.where(is_cosine, cos_at, -sin_at)
            by_sine = jnp.where(is_cosine, -sin_at, -cos_at)
            value = cosine * by_cosine + sine * by_sine
            high = value.astype(jnp.bfloat16)
            high_ref[pl.ds(base, step), at * width : (at + 1) * width] = high
            rest_ref[pl.ds(base, step), at * width : (at + 1) * width] = (
                value - high.astype(jnp.float32)
            ).astype(jnp.bfloat16)

    if columns <= 256:
        for base in range(0, columns, step):
            fill(base)
    else:

        @pl.loop(0, columns // step)
        def _(at):
            fill(pl.multiple_of(at * step, step))


def synthesis_kernel(
    dims,
    low_ref,
    rate_ref,
    coupling_ref,
    state_ref,
    table_ref,
    out_ref,
    high_ref,
    rest_ref,
    factor_ref,
    spread_ref,
):
    pairs_dev, block, mode_count, orders_total = dims
    fields = state_ref.shape[1]
    rows_total = state_ref.shape[-1]
    chunk_rows = out_ref.shape[0] // mode_count
    group = lax.axis_index("mode") * pairs_dev
    pieces = []
    for pair in range(pairs_dev):
        lower = own_lower(low_ref, group + pair)
        members, signs = row_factors(lower, (1, rows_total), orders_total)
        coeffs = [state_rows(state_ref, pair, part, (*range(fields), 0)) for part in range(2)]
        left = []
        for k in range(2):
            order = lower if k == 0 else orders_total - 1 - lower
            weight = jnp.where(order == 0, 1.0, 2.0)
            member = jnp.where(members[k], weight, 0.0)
            for part in range(2):
                left.append(coeffs[part] * member)
                left.append(coeffs[part] * (member * signs[k]))
        left = jnp.concatenate(left, axis=0).astype(jnp.bfloat16)
        pieces.append(jnp.dot(left, table_ref[pair], preferred_element_type=jnp.float32))
    fourier = jnp.concatenate(pieces, axis=0).astype(jnp.bfloat16).astype(jnp.float32)
    turned = fourier.T
    lane_block = lax.broadcasted_iota(jnp.int32, (mode_count, LANES), 1) // block
    count = turned.shape[0] // mode_count
    for row in range(chunk_rows):
        merged = jnp.zeros((mode_count, LANES), jnp.float32)
        for i in range(count):
            part = turned[i * mode_count : (i + 1) * mode_count]
            moved = pltpu.roll(part, (block * (i - row)) % LANES, 1)
            merged = jnp.where(lane_block == i, moved, merged)
        spread_ref[:, row, :] = merged
    out_ref[...] = spread_ref[...].reshape(out_ref.shape).astype(jnp.bfloat16)
    rows = factor_ref.shape[1]
    at = lax.broadcasted_iota(jnp.int32, (rows, LANES), 0) // (rows // (fields + 1))
    for k, ref in enumerate((rate_ref, coupling_ref)):
        values = ref[...][None, :]
        factor = jnp.broadcast_to(values[:, 0:1], (rows, LANES))
        factor = jnp.where(at == 1, values[:, 2:3], factor)
        factor_ref[k] = jnp.where(at == 2, values[:, 1:2], factor)
    fill_waves(low_ref[...][None, :].astype(jnp.float32), orders_total, high_ref, rest_ref, 32)


def product_kernel(dims, sent_ref, high_ref, rest_ref, out_ref):
    used, shells, scale = dims
    turned = sent_ref[...].astype(jnp.float32).T[:used].astype(jnp.bfloat16)
    grid = jnp.dot(turned, high_ref[...], preferred_element_type=jnp.float32)
    grid = grid + jnp.dot(turned, rest_ref[...], preferred_element_type=jnp.float32)
    products = grid * pltpu.roll(grid, used - shells, 0)
    high = products.astype(jnp.bfloat16)
    rest = (products - high.astype(jnp.float32)).astype(jnp.bfloat16)
    both = lax.dot_general(
        high_ref[...], jnp.concatenate([high, rest], axis=0), NT, preferred_element_type=jnp.float32
    )
    totals = lax.dot_general(rest_ref[...], high, NT, preferred_element_type=jnp.float32)
    totals = totals + both[:, :used] + both[:, used:]
    answers = (totals * scale).astype(jnp.bfloat16)
    out_ref[...] = jnp.concatenate(
        [answers, jnp.zeros((answers.shape[0], LANES - used), jnp.bfloat16)], axis=1
    )


def analysis_sums(dims, low_ref, sent_ref, table_ref, spread_ref, emit):
    pairs_dev, block, count, mode_count, orders_total = dims
    rows_total = table_ref.shape[1]
    chunk_rows = sent_ref.shape[0] // mode_count
    group = lax.axis_index("mode") * pairs_dev
    spread_ref[...] = sent_ref[...].astype(jnp.float32).reshape(spread_ref.shape)
    lane_block = lax.broadcasted_iota(jnp.int32, (mode_count, LANES), 1) // block
    parts = [jnp.zeros((mode_count, LANES), jnp.float32) for _ in range(count)]
    for row in range(chunk_rows):
        piece = spread_ref[:, row, :]
        for i in range(count):
            moved = pltpu.roll(piece, (block * (row - i)) % LANES, 1)
            parts[i] = jnp.where(lane_block == row, moved, parts[i])
    returned = jnp.concatenate(parts, axis=0).T.astype(jnp.bfloat16)
    per_pair = returned.shape[0] // pairs_dev
    half = block // 2
    for pair in range(pairs_dev):
        lower = own_lower(low_ref, group + pair)
        members, signs = row_factors(lower, (1, rows_total), orders_total)
        sums = lax.dot_general(
            returned[pair * per_pair : (pair + 1) * per_pair],
            table_ref[pair],
            NT,
            preferred_element_type=jnp.float32,
        )
        for part in range(2):
            total = jnp.zeros((half, rows_total), jnp.float32)
            for k in range(2):
                at = (k * 2 + part) * block
                north = sums[at : at + half]
                south = sums[at + half : at + block]
                total = jnp.where(members[k], north + signs[k] * south, total)
            emit(pair, part, lower, total)


def analysis_kernel(dims, low_ref, sent_ref, table_ref, out_ref, spread_ref):
    def emit(pair, part, lower, total):
        out_ref[pair, part] = total

    analysis_sums(dims, low_ref, sent_ref, table_ref, spread_ref, emit)


def step_kernel(
    dims, low_ref, factor_ref, sent_ref, table_ref, state_ref, out_ref, spread_ref
):
    orders_total = dims[-1]
    rows_total = table_ref.shape[1]
    half = dims[1] // 2
    fields = (0, 2, 1, 0)
    at = lax.broadcasted_iota(jnp.int32, (half, 1), 0)
    upper = at % 2 == 1
    def other(value):
        return jnp.where(upper, pltpu.roll(value, 1, 0), pltpu.roll(value, half - 1, 0))

    rate = factor_ref[0, :, 0:1]
    strength = factor_ref[1, :, 0:1]
    radius = inner_radius + (jnp.where(upper, 1.0, 0.0) + 0.5) * shell_step
    inverse = (shell_step * shell_step) / (radius * radius)
    row = lax.broadcasted_iota(jnp.int32, (1, rows_total), 1)
    cache = {}

    def emit(pair, part, lower, total):
        if pair not in cache:
            degree = jnp.where(row < orders_total - lower, lower + row, row - 1).astype(jnp.float32)
            damping = (degree * (degree + 1.0)) * inverse
            diagonal = 1.0 + rate * (2.0 + damping)
            crossed = other(diagonal)
            factor = 1.0 / (diagonal * crossed - rate * rate)
            cache[pair] = (damping, crossed * factor, rate * factor)
        damping, own, across = cache[pair]
        state = state_rows(state_ref, pair, part, fields)
        laplace = other(state) - 2.0 * state - damping * state
        drive = state + rate * (laplace + strength * total)
        updated = own * drive + across * other(drive)
        for k, f in enumerate(fields[:3]):
            for s in range(2):
                out_ref[pair, f, s, part : part + 1, :] = updated[2 * k + s : 2 * k + s + 1]

    analysis_sums(dims, low_ref, sent_ref, table_ref, spread_ref, emit)


def vmem(count):
    return [pl.BlockSpec(memory_space=pltpu.VMEM)] * count


def body(spectral_state, synthesis_table, low_orders, diffusion, coupling):
    radial_count = lax.axis_size("radial")
    if radial_count > 1:
        synthesis_table = lax.all_gather(synthesis_table, "radial", axis=2, tiled=True)
    pairs_dev, field_count, shell_count, part_count, rows_total = spectral_state.shape
    half_lat = synthesis_table.shape[2]
    lat_total = 2 * half_lat
    orders_total = rows_total - 1
    lon_total = 3 * orders_total
    mode_count = lax.axis_size("mode")
    chunk_rows = pairs_dev * 2 * part_count
    column_count = chunk_rows * mode_count
    count = half_lat // mode_count
    half = (field_count + 1) * shell_count
    block = 2 * half
    used = count * block
    assert half == 8 and chunk_rows * block == LANES and used <= LANES // 2 and part_count == 2
    scale = 2.0 * math.sqrt(orders_total * rows_total / (lat_total * lon_total))
    spread = pltpu.VMEM((mode_count, chunk_rows, LANES), jnp.float32)
    sent = jax.ShapeDtypeStruct((column_count, LANES), jnp.bfloat16)
    table_shape = jax.ShapeDtypeStruct((column_count, lon_total), jnp.bfloat16)
    factor_shape = jax.ShapeDtypeStruct((2, half, LANES), jnp.float32)
    chunks, wave_high, wave_rest, factors = pl.pallas_call(
        functools.partial(synthesis_kernel, (pairs_dev, block, mode_count, orders_total)),
        out_shape=[sent, table_shape, table_shape, factor_shape],
        in_specs=vmem(5),
        out_specs=vmem(4),
        scratch_shapes=[spread],
        compiler_params=GRANT,
        name="synthesis",
    )(low_orders, diffusion, coupling, spectral_state, synthesis_table)
    pieces = lax.all_to_all(chunks, "mode", split_axis=0, concat_axis=0, tiled=True)
    answers = pl.pallas_call(
        functools.partial(product_kernel, (used, shell_count, scale)),
        out_shape=sent,
        in_specs=vmem(3),
        out_specs=pl.BlockSpec(memory_space=pltpu.VMEM),
        compiler_params=GRANT,
        name="products",
    )(pieces, wave_high, wave_rest)
    returned = lax.all_to_all(answers, "mode", split_axis=0, concat_axis=0, tiled=True)
    dims = (pairs_dev, block, count, mode_count, orders_total)
    if radial_count == 1 and shell_count == 2:
        return pl.pallas_call(
            functools.partial(step_kernel, dims),
            out_shape=jax.ShapeDtypeStruct(spectral_state.shape, jnp.float32),
            in_specs=vmem(5),
            out_specs=pl.BlockSpec(memory_space=pltpu.VMEM),
            scratch_shapes=[spread],
            compiler_params=GRANT,
            name="step",
        )(low_orders, factors, returned, synthesis_table, spectral_state)
    nonlinear = pl.pallas_call(
        functools.partial(analysis_kernel, dims),
        out_shape=jax.ShapeDtypeStruct((pairs_dev, part_count, half, rows_total), jnp.float32),
        in_specs=vmem(3),
        out_specs=pl.BlockSpec(memory_space=pltpu.VMEM),
        scratch_shapes=[spread],
        compiler_params=GRANT,
        name="analysis",
    )(low_orders, returned, synthesis_table)
    nonlinear = nonlinear.reshape(pairs_dev, part_count, field_count + 1, shell_count, rows_total)
    nonlinear = jnp.stack([nonlinear[:, :, 0], nonlinear[:, :, 2], nonlinear[:, :, 1]], axis=1)
    nonlinear = nonlinear.transpose(0, 1, 3, 2, 4)
    return solve(spectral_state, nonlinear, low_orders, diffusion, coupling)


def solve(spectral_state, nonlinear, low_orders, diffusion, coupling):
    pairs_dev, field_count, shell_count, part_count, rows_total = spectral_state.shape
    orders_total = rows_total - 1
    radial_count = lax.axis_size("radial")
    own = lax.dynamic_slice_in_dim(low_orders, lax.axis_index("mode") * pairs_dev, pairs_dev)
    row_index = lax.iota(jnp.int32, rows_total)[None, :]
    lower_col = own[:, None]
    degree = jnp.where(row_index < orders_total - lower_col, lower_col + row_index, row_index - 1)
    radial_at = lax.axis_index("radial")
    rate_col = diffusion.reshape(1, field_count, 1, 1)
    strength = coupling.reshape(1, field_count, 1, 1)
    degree_term = degree.astype(jnp.float32)
    degree_term = (degree_term * (degree_term + 1.0))[:, None, None, :] * (shell_step * shell_step)
    if radial_count > 1:
        with_edges = with_halo(spectral_state, "radial", 2, 1)
    else:
        with_edges = jnp.pad(spectral_state, ((0, 0), (0, 0), (1, 1), (0, 0), (0, 0)))
    diagonals = []
    drives = []
    for shell_at in range(shell_count):
        radius = (
            inner_radius
            + ((radial_at * shell_count + shell_at).astype(jnp.float32) + 0.5) * shell_step
        )
        damping = degree_term / (radius * radius)
        middle = with_edges[:, :, shell_at + 1]
        laplace = (
            with_edges[:, :, shell_at + 2]
            - 2.0 * middle
            + with_edges[:, :, shell_at]
            - damping * middle
        )
        drives.append(middle + rate_col * (laplace + strength * nonlinear[:, :, shell_at]))
        diagonals.append(1.0 + rate_col * (2.0 + damping))
    narrow_zero = jnp.zeros(diagonals[0].shape, jnp.float32)
    wide_zero = jnp.zeros(drives[0].shape, jnp.float32)
    pivot_prev = narrow_zero
    carry_u, carry_v, carry_w = (wide_zero, narrow_zero, narrow_zero)
    pivots, sweep_u, sweep_v, sweep_w = ([], [], [], [])
    for shell_at in range(shell_count):
        denom_at = diagonals[shell_at] + rate_col * pivot_prev
        pivot_prev = -rate_col / denom_at
        first_drive = rate_col if shell_at == 0 else 0.0
        last_drive = rate_col if shell_at == shell_count - 1 else 0.0
        carry_u = (drives[shell_at] + rate_col * carry_u) / denom_at
        carry_v = (first_drive + rate_col * carry_v) / denom_at
        carry_w = (last_drive + rate_col * carry_w) / denom_at
        pivots.append(pivot_prev)
        sweep_u.append(carry_u)
        sweep_v.append(carry_v)
        sweep_w.append(carry_w)
    solved_u, solved_v, solved_w = ([sweep_u[-1]], [sweep_v[-1]], [sweep_w[-1]])
    for shell_at in range(shell_count - 2, -1, -1):
        solved_u.insert(0, sweep_u[shell_at] - pivots[shell_at] * solved_u[0])
        solved_v.insert(0, sweep_v[shell_at] - pivots[shell_at] * solved_v[0])
        solved_w.insert(0, sweep_w[shell_at] - pivots[shell_at] * solved_w[0])
    if radial_count == 1:
        return jnp.stack(solved_u, axis=2)
    first_u, last_u = (solved_u[0], solved_u[-1])
    first_v, last_v = (solved_v[0], solved_v[-1])
    first_w, last_w = (solved_w[0], solved_w[-1])
    wide_rows = jnp.stack([first_u, last_u])[None]
    narrow_rows = jnp.stack([first_v, first_w, last_v, last_w])[None]
    wide_all, narrow_all = (
        lax.all_gather(wide_rows, "radial", axis=0, tiled=True),
        lax.all_gather(narrow_rows, "radial", axis=0, tiled=True),
    )
    chain_count = lax.axis_size("radial")
    alpha_now, beta_now = (wide_zero, narrow_zero)
    alphas, betas = ([], [])
    for member in range(chain_count):
        alphas.append(alpha_now)
        betas.append(beta_now)
        peer_first_u, peer_last_u = (wide_all[member, 0], wide_all[member, 1])
        peer_first_v, peer_first_w = (narrow_all[member, 0], narrow_all[member, 1])
        peer_last_v, peer_last_w = (narrow_all[member, 2], narrow_all[member, 3])
        shrink = 1.0 - peer_first_v * beta_now
        alpha_new = (
            peer_last_u
            - peer_last_u * peer_first_v * beta_now
            + peer_last_v * alpha_now
            + peer_last_v * peer_first_u * beta_now
        ) / shrink
        beta_new = (
            peer_last_w
            - peer_last_w * peer_first_v * beta_now
            + peer_last_v * peer_first_w * beta_now
        ) / shrink
        alpha_now, beta_now = (alpha_new, beta_new)
    next_first = wide_zero
    firsts = [None] * chain_count
    nexts = [None] * chain_count
    for member in range(chain_count - 1, -1, -1):
        nexts[member] = next_first
        peer_first_u = wide_all[member, 0]
        peer_first_v, peer_first_w = (narrow_all[member, 0], narrow_all[member, 1])
        next_first = (peer_first_u + peer_first_v * alphas[member] + peer_first_w * next_first) / (
            1.0 - peer_first_v * betas[member]
        )
        firsts[member] = next_first
    alpha_prev = lax.dynamic_index_in_dim(jnp.stack(alphas), radial_at, 0, keepdims=False)
    beta_prev = lax.dynamic_index_in_dim(jnp.stack(betas), radial_at, 0, keepdims=False)
    own_first = lax.dynamic_index_in_dim(jnp.stack(firsts), radial_at, 0, keepdims=False)
    next_first = lax.dynamic_index_in_dim(jnp.stack(nexts), radial_at, 0, keepdims=False)
    prev_last = alpha_prev + beta_prev * own_first
    outputs = []
    for shell_at in range(shell_count):
        outputs.append(
            solved_u[shell_at] + prev_last * solved_v[shell_at] + next_first * solved_w[shell_at]
        )
    return jnp.stack(outputs, axis=2)


def solution(mesh):
    placed = (P("mode", None, "radial", None, None), P("mode", None, "radial"), P(), P(), P())
    return jax.shard_map(
        body,
        mesh=mesh,
        in_specs=placed,
        out_specs=P("mode", None, "radial", None, None),
        check_vma=False,
    )
```

```python
import functools
import math

import jax
import jax.numpy as jnp
from jax import lax
from jax.experimental import pallas as pl
from jax.experimental.pallas import tpu as pltpu
from jax.sharding import PartitionSpec as P

inner_radius = 0.538
shell_step = 1.0 / 2048.0
LANES = 128
GRANT = pltpu.CompilerParams(vmem_limit_bytes=16 * 1024 * 1024)
NT = (((1,), (1,)), ((), ()))


def with_halo(shard, axis, dim, width):
    count, length = (lax.axis_size(axis), shard.shape[dim])
    up = [(i, (i + 1) % count) for i in range(count - 1)]
    down = [(j, i) for i, j in up]
    last = lax.slice_in_dim(shard, length - width, length, axis=dim)
    first = lax.slice_in_dim(shard, 0, width, axis=dim)
    before = lax.ppermute(last, axis, up)
    after = lax.ppermute(first, axis, down)
    return jnp.concatenate([before, shard, after], axis=dim)


def own_lower(low_ref, at):
    low_row = low_ref[...][None, :]
    lane = lax.broadcasted_iota(jnp.int32, low_row.shape, 1)
    return jnp.sum(jnp.where(lane == at, low_row, 0), axis=1, keepdims=True)


def row_factors(lower, shape, orders_total):
    row = lax.broadcasted_iota(jnp.int32, shape, len(shape) - 1)
    in_lower = row < orders_total - lower
    odd_lower = lax.rem(row, 2) == 1
    odd_upper = lax.rem(row + orders_total - lower, 2) == 1
    members = (in_lower, jnp.logical_not(in_lower))
    signs = (jnp.where(odd_lower, -1.0, 1.0), jnp.where(odd_upper, -1.0, 1.0))
    return members, signs


def state_rows(state_ref, pair, part, fields):
    shells = state_ref.shape[2]
    rows = [state_ref[pair, f, s, part : part + 1, :] for f in fields for s in range(shells)]
    return jnp.concatenate(rows, axis=0)


def fill_waves(low_row, orders_total, high_ref, rest_ref, step):
    columns, lon_total = high_ref.shape
    width = lon_total // 3
    lon = lax.broadcasted_iota(jnp.int32, (step, width), 1).astype(jnp.float32)
    pair_lane = lax.broadcasted_iota(jnp.int32, (step, low_row.shape[1]), 1)
    third = math.sqrt(0.75)

    def fill(base):
        column = base + lax.broadcasted_iota(jnp.int32, (step, 1), 0)
        hit = pair_lane == column // 4
        lower = jnp.sum(jnp.where(hit, low_row, 0.0), axis=1, keepdims=True)
        is_lower = (column // 2) % 2 == 0
        is_cosine = column % 2 == 0
        order = jnp.where(is_lower, lower, orders_total - 1 - lower)
        turns = order * lon
        quad = jnp.floor(turns * (4.0 / lon_total) + 0.5)
        angle = (turns - quad * (lon_total / 4)) * (2.0 * math.pi / lon_total)
        square = angle * angle
        cosine = 1.0 + square * (
            -0.5 + square * (1.0 / 24 + square * (-1.0 / 720 + square * (1.0 / 40320)))
        )
        sine = 1.0 / 120 + square * (-1.0 / 5040 + square * (1.0 / 362880))
        sine = angle * (1.0 + square * (-1.0 / 6 + square * sine))
        quad = quad.astype(jnp.int32)
        swap = (quad & 1) == 1
        cosine, sine = (jnp.where(swap, sine, cosine), jnp.where(swap, cosine, sine))
        cosine = jnp.where(((quad + 1) & 2) == 2, -cosine, cosine)
        sine = jnp.where((quad & 2) == 2, -sine, sine)
        for at in range(3):
            turn = at * order
            turn = turn - 3.0 * jnp.floor((turn + 0.5) * (1.0 / 3.0))
            cos_at = jnp.where(turn == 0.0, 1.0, -0.5)
            sin_at = jnp.where(turn == 0.0, 0.0, jnp.where(turn == 1.0, third, -third))
            by_cosine = jnp.where(is_cosine, cos_at, -sin_at)
            by_sine = jnp.where(is_cosine, -sin_at, -cos_at)
            value = cosine * by_cosine + sine * by_sine
            high = value.astype(jnp.bfloat16)
            high_ref[pl.ds(base, step), at * width : (at + 1) * width] = high
            rest_ref[pl.ds(base, step), at * width : (at + 1) * width] = (
                value - high.astype(jnp.float32)
            ).astype(jnp.bfloat16)

    if columns <= 256:
        for base in range(0, columns, step):
            fill(base)
    else:

        @pl.loop(0, columns // step)
        def _(at):
            fill(pl.multiple_of(at * step, step))


def synthesis_kernel(
    dims,
    low_ref,
    rate_ref,
    coupling_ref,
    state_ref,
    table_ref,
    out_ref,
    high_ref,
    rest_ref,
    factor_ref,
    spread_ref,
):
    pairs_dev, block, mode_count, orders_total = dims
    fields = state_ref.shape[1]
    rows_total = state_ref.shape[-1]
    chunk_rows = out_ref.shape[0] // mode_count
    group = lax.axis_index("mode") * pairs_dev
    pieces = []
    for pair in range(pairs_dev):
        lower = own_lower(low_ref, group + pair)
        members, signs = row_factors(lower, (1, rows_total), orders_total)
        coeffs = [state_rows(state_ref, pair, part, (*range(fields), 0)) for part in range(2)]
        left = []
        for k in range(2):
            order = lower if k == 0 else orders_total - 1 - lower
            weight = jnp.where(order == 0, 1.0, 2.0)
            member = jnp.where(members[k], weight, 0.0)
            for part in range(2):
                left.append(coeffs[part] * member)
                left.append(coeffs[part] * (member * signs[k]))
        left = jnp.concatenate(left, axis=0).astype(jnp.bfloat16)
        pieces.append(jnp.dot(left, table_ref[pair], preferred_element_type=jnp.float32))
    fourier = jnp.concatenate(pieces, axis=0).astype(jnp.bfloat16).astype(jnp.float32)
    turned = fourier.T
    lane_block = lax.broadcasted_iota(jnp.int32, (mode_count, LANES), 1) // block
    count = turned.shape[0] // mode_count
    for row in range(chunk_rows):
        merged = jnp.zeros((mode_count, LANES), jnp.float32)
        for i in range(count):
            part = turned[i * mode_count : (i + 1) * mode_count]
            moved = pltpu.roll(part, (block * (i - row)) % LANES, 1)
            merged = jnp.where(lane_block == i, moved, merged)
        spread_ref[:, row, :] = merged
    out_ref[...] = spread_ref[...].reshape(out_ref.shape).astype(jnp.bfloat16)
    rows = factor_ref.shape[1]
    at = lax.broadcasted_iota(jnp.int32, (rows, LANES), 0) // (rows // (fields + 1))
    for k, ref in enumerate((rate_ref, coupling_ref)):
        values = ref[...][None, :]
        factor = jnp.broadcast_to(values[:, 0:1], (rows, LANES))
        factor = jnp.where(at == 1, values[:, 2:3], factor)
        factor_ref[k] = jnp.where(at == 2, values[:, 1:2], factor)
    fill_waves(low_ref[...][None, :].astype(jnp.float32), orders_total, high_ref, rest_ref, 32)


def product_kernel(dims, sent_ref, high_ref, rest_ref, out_ref):
    used, shells, scale = dims
    turned = sent_ref[...].astype(jnp.float32).T[:used].astype(jnp.bfloat16)
    grid = jnp.dot(turned, high_ref[...], preferred_element_type=jnp.float32)
    grid = grid + jnp.dot(turned, rest_ref[...], preferred_element_type=jnp.float32)
    products = grid * pltpu.roll(grid, used - shells, 0)
    high = products.astype(jnp.bfloat16)
    rest = (products - high.astype(jnp.float32)).astype(jnp.bfloat16)
    both = lax.dot_general(
        high_ref[...], jnp.concatenate([high, rest], axis=0), NT, preferred_element_type=jnp.float32
    )
    totals = lax.dot_general(rest_ref[...], high, NT, preferred_element_type=jnp.float32)
    totals = totals + both[:, :used] + both[:, used:]
    answers = (totals * scale).astype(jnp.bfloat16)
    out_ref[...] = jnp.concatenate(
        [answers, jnp.zeros((answers.shape[0], LANES - used), jnp.bfloat16)], axis=1
    )


def analysis_sums(dims, low_ref, sent_ref, table_ref, spread_ref, emit):
    pairs_dev, block, count, mode_count, orders_total = dims
    rows_total = table_ref.shape[1]
    chunk_rows = sent_ref.shape[0] // mode_count
    group = lax.axis_index("mode") * pairs_dev
    spread_ref[...] = sent_ref[...].astype(jnp.float32).reshape(spread_ref.shape)
    lane_block = lax.broadcasted_iota(jnp.int32, (mode_count, LANES), 1) // block
    parts = [jnp.zeros((mode_count, LANES), jnp.float32) for _ in range(count)]
    for row in range(chunk_rows):
        piece = spread_ref[:, row, :]
        for i in range(count):
            moved = pltpu.roll(piece, (block * (row - i)) % LANES, 1)
            parts[i] = jnp.where(lane_block == row, moved, parts[i])
    returned = jnp.concatenate(parts, axis=0).T.astype(jnp.bfloat16)
    per_pair = returned.shape[0] // pairs_dev
    half = block // 2
    for pair in range(pairs_dev):
        lower = own_lower(low_ref, group + pair)
        members, signs = row_factors(lower, (1, rows_total), orders_total)
        sums = lax.dot_general(
            returned[pair * per_pair : (pair + 1) * per_pair],
            table_ref[pair],
            NT,
            preferred_element_type=jnp.float32,
        )
        for part in range(2):
            total = jnp.zeros((half, rows_total), jnp.float32)
            for k in range(2):
                at = (k * 2 + part) * block
                north = sums[at : at + half]
                south = sums[at + half : at + block]
                total = jnp.where(members[k], north + signs[k] * south, total)
            emit(pair, part, lower, total)


def analysis_kernel(dims, low_ref, sent_ref, table_ref, out_ref, spread_ref):
    def emit(pair, part, lower, total):
        out_ref[pair, part] = total

    analysis_sums(dims, low_ref, sent_ref, table_ref, spread_ref, emit)


def step_kernel(
    dims, low_ref, factor_ref, sent_ref, table_ref, state_ref, out_ref, spread_ref
):
    orders_total = dims[-1]
    rows_total = table_ref.shape[1]
    half = dims[1] // 2
    fields = (0, 2, 1, 0)
    at = lax.broadcasted_iota(jnp.int32, (half, 1), 0)
    upper = at % 2 == 1
    def other(value):
        return jnp.where(upper, pltpu.roll(value, 1, 0), pltpu.roll(value, half - 1, 0))

    rate = factor_ref[0, :, 0:1]
    strength = factor_ref[1, :, 0:1]
    radius = inner_radius + (jnp.where(upper, 1.0, 0.0) + 0.5) * shell_step
    inverse = (shell_step * shell_step) / (radius * radius)
    row = lax.broadcasted_iota(jnp.int32, (1, rows_total), 1)
    cache = {}

    def emit(pair, part, lower, total):
        if pair not in cache:
            degree = jnp.where(row < orders_total - lower, lower + row, row - 1).astype(jnp.float32)
            damping = (degree * (degree + 1.0)) * inverse
            diagonal = 1.0 + rate * (2.0 + damping)
            crossed = other(diagonal)
            factor = 1.0 / (diagonal * crossed - rate * rate)
            cache[pair] = (damping, crossed * factor, rate * factor)
        damping, own, across = cache[pair]
        state = state_rows(state_ref, pair, part, fields)
        laplace = other(state) - 2.0 * state - damping * state
        drive = state + rate * (laplace + strength * total)
        updated = own * drive + across * other(drive)
        for k, f in enumerate(fields[:3]):
            for s in range(2):
                out_ref[pair, f, s, part : part + 1, :] = updated[2 * k + s : 2 * k + s + 1]

    analysis_sums(dims, low_ref, sent_ref, table_ref, spread_ref, emit)


def vmem(count):
    return [pl.BlockSpec(memory_space=pltpu.VMEM)] * count


def row_lower(low_ref, first, rows, pairs_dev):
    at = lax.broadcasted_iota(jnp.int32, (rows, 1), 0)
    lower = jnp.zeros((rows, 1), jnp.int32)
    for pair in range(pairs_dev):
        lower = jnp.where(at // (rows // pairs_dev) == pair, own_lower(low_ref, first + pair), lower)
    return at, lower


def row_members(at, lower, rows_total, orders_total):
    row = lax.broadcasted_iota(jnp.int32, (1, rows_total), 1)
    upper = (at // 2) % 2 == 1
    edge = orders_total - lower
    member = jnp.logical_xor(row < edge, upper)
    odd = ((row + jnp.where(upper, edge, 0)) & 1) == 1
    return member, odd


def paired_state(state_ref, field, shell):
    pairs_dev = state_ref.shape[0]
    pieces = [state_ref[pair, field, shell] for pair in range(pairs_dev) for _ in range(2)]
    return jnp.concatenate(pieces, axis=0)


def wave_values(turns, lon_total):
    quad = jnp.floor(turns * (4.0 / lon_total) + 0.5)
    angle = (turns - quad * (lon_total / 4)) * (2.0 * math.pi / lon_total)
    square = angle * angle
    cosine = 1.0 + square * (
        -0.5 + square * (1.0 / 24 + square * (-1.0 / 720 + square * (1.0 / 40320)))
    )
    sine = 1.0 / 120 + square * (-1.0 / 5040 + square * (1.0 / 362880))
    sine = angle * (1.0 + square * (-1.0 / 6 + square * sine))
    quad = quad.astype(jnp.int32)
    swap = (quad & 1) == 1
    cosine, sine = (jnp.where(swap, sine, cosine), jnp.where(swap, cosine, sine))
    cosine = jnp.where(((quad + 1) & 2) == 2, -cosine, cosine)
    sine = jnp.where((quad & 2) == 2, -sine, sine)
    return cosine, sine


def third_factors(order, is_cosine, at):
    third = math.sqrt(0.75)
    turn = at * order
    turn = turn - 3.0 * jnp.floor((turn + 0.5) * (1.0 / 3.0))
    cos_at = jnp.where(turn == 0.0, 1.0, -0.5)
    sin_at = jnp.where(turn == 0.0, 0.0, jnp.where(turn == 1.0, third, -third))
    by_cosine = jnp.where(is_cosine, cos_at, -sin_at)
    by_sine = jnp.where(is_cosine, -sin_at, -cos_at)
    return by_cosine, by_sine


def two_terms(value):
    high = value.astype(jnp.bfloat16)
    return high, (value - high.astype(jnp.float32)).astype(jnp.bfloat16)


def band_synthesis_kernel(
    dims,
    low_ref,
    rate_ref,
    coupling_ref,
    state_ref,
    table_ref,
    out_ref,
    high_ref,
    rest_ref,
    own_ref,
    factor_ref,
):
    group, mode_count, orders_total = dims
    pairs_dev, fields, shells, _, rows_total = state_ref.shape
    rows = out_ref.shape[0] // mode_count
    me = lax.axis_index("mode")
    at, lower = row_lower(low_ref, me * pairs_dev, rows, pairs_dev)
    member, odd = row_members(at, lower, rows_total, orders_total)
    order = jnp.where((at // 2) % 2 == 1, orders_total - 1 - lower, lower)
    weight = jnp.where(order == 0, 1.0, 2.0)
    north = jnp.where(member, weight, 0.0)
    south = jnp.where(odd, -north, north)
    state = [[paired_state(state_ref, f, s) for f in range(fields)] for s in range(shells)]
    fourier = None
    for pair in range(pairs_dev):
        mine = at // (rows // pairs_dev) == pair
        left = [
            state[s][f] * jnp.where(mine, factor, 0.0)
            for factor in (north, south)
            for s in range(shells)
            for f in range(fields)
        ]
        left = jnp.concatenate(left, axis=0).astype(jnp.bfloat16)
        part = jnp.dot(left, table_ref[pair], preferred_element_type=jnp.float32)
        fourier = part if fourier is None else fourier + part
    fourier = fourier.astype(jnp.bfloat16).astype(jnp.float32)
    width = LANES // group
    lane_block = lax.broadcasted_iota(jnp.int32, (fields * rows, LANES), 1) // width
    for band in range(group):
        piece = None
        for block in range(group):
            source = fourier[block * fields * rows : (block + 1) * fields * rows]
            moved = pltpu.roll(source, (width * (block - band)) % LANES, 1)
            piece = moved if piece is None else jnp.where(lane_block == block, moved, piece)
        for field in range(fields):
            value = piece[field * rows : (field + 1) * rows].astype(jnp.bfloat16)
            for device in range(band, mode_count, group):
                out_ref[device * rows : (device + 1) * rows, field * LANES : (field + 1) * LANES] = value

    lon_total, columns = high_ref.shape
    span = lon_total // 3
    low_row = low_ref[...][None, :].astype(jnp.float32)
    pair_at = lax.broadcasted_iota(jnp.int32, (low_row.shape[1], columns), 0)
    column = lax.broadcasted_iota(jnp.int32, (low_row.shape[1], columns), 1)
    spread = jnp.where(column // 4 == pair_at, 1.0, 0.0).astype(jnp.bfloat16)
    lowers = jnp.broadcast_to(low_row, (8, low_row.shape[1])).astype(jnp.bfloat16)
    lowers = jnp.dot(lowers, spread, preferred_element_type=jnp.float32)[0:1]
    column = lax.broadcasted_iota(jnp.int32, (1, columns), 1)
    orders = jnp.where((column // 2) % 2 == 0, lowers, orders_total - 1 - lowers)
    is_cosine = column % 2 == 0
    factors = [third_factors(orders, is_cosine, third) for third in range(3)]
    step = min(span, 32)
    for base in range(0, span, step):
        lon = (base + lax.broadcasted_iota(jnp.int32, (step, 1), 0)).astype(jnp.float32)
        cosine, sine = wave_values(lon * orders, lon_total)
        for third, (by_cosine, by_sine) in enumerate(factors):
            high, rest = two_terms(cosine * by_cosine + sine * by_sine)
            high_ref[third * span + base : third * span + base + step, :] = high
            rest_ref[third * span + base : third * span + base + step, :] = rest
    count = group * rows
    at = lax.broadcasted_iota(jnp.int32, (count, 1), 0)
    device = me - me % group + ((me % group) ^ (at // rows))
    pair_index = device * pairs_dev + (at % rows) // 4
    pair_lane = lax.broadcasted_iota(jnp.int32, (count, low_row.shape[1]), 1)
    lowers = jnp.sum(jnp.where(pair_lane == pair_index, low_row, 0.0), axis=1, keepdims=True)
    orders = jnp.where((at // 2) % 2 == 0, lowers, orders_total - 1 - lowers)
    is_cosine = at % 2 == 0
    lon = lax.broadcasted_iota(jnp.int32, (1, span), 1).astype(jnp.float32)
    cosine, sine = wave_values(lon * orders, lon_total)
    for third in range(3):
        by_cosine, by_sine = third_factors(orders, is_cosine, third)
        high, rest = two_terms(cosine * by_cosine + sine * by_sine)
        own_ref[:count, third * span : (third + 1) * span] = high
        own_ref[count:, third * span : (third + 1) * span] = rest
    for k, ref in enumerate((rate_ref, coupling_ref)):
        for f in range(fields):
            factor_ref[k, f] = jnp.broadcast_to(ref[...][None, f : f + 1], (8, LANES))


def band_product_kernel(scale, sent_ref, high_ref, rest_ref, own_ref, *out_refs):
    sent = sent_ref[...]
    grid = jnp.dot(high_ref[...], sent, preferred_element_type=jnp.float32)
    grid = grid + jnp.dot(rest_ref[...], sent, preferred_element_type=jnp.float32)
    width = sent.shape[1] // 3
    first, second, third = (grid[:, f * width : (f + 1) * width] for f in range(3))
    products = jnp.concatenate([first * second, first * third, second * third], axis=1)
    high, rest = two_terms(products)
    count = own_ref.shape[0] // 2
    both = jnp.dot(own_ref[...], high, preferred_element_type=jnp.float32)
    totals = jnp.dot(own_ref[:count], rest, preferred_element_type=jnp.float32)
    totals = totals + both[:count] + both[count:]
    answers = (totals * scale).astype(jnp.bfloat16)
    rows = count // len(out_refs)
    for at, out_ref in enumerate(out_refs):
        out_ref[...] = answers[at * rows : (at + 1) * rows]


def band_step_kernel(dims, low_ref, factor_ref, state_ref, table_ref, *refs):
    group, orders_total = dims
    sent_refs, out_ref = (refs[:group], refs[group])
    pairs_dev, fields, shells, _, rows_total = state_ref.shape
    rows = sent_refs[0].shape[0]
    me = lax.axis_index("mode")
    at, lower = row_lower(low_ref, me * pairs_dev, rows, pairs_dev)
    member, odd = row_members(at, lower, rows_total, orders_total)
    width = LANES // group
    lane_block = lax.broadcasted_iota(jnp.int32, (fields * rows, LANES), 1) // width
    pieces = []
    for ref in sent_refs:
        value = ref[...].astype(jnp.float32)
        pieces.append(
            jnp.concatenate([value[:, f * LANES : (f + 1) * LANES] for f in range(fields)], axis=0)
        )
    returned = []
    for block in range(group):
        merged = jnp.zeros((fields * rows, LANES), jnp.float32)
        for mask, piece in enumerate(pieces):
            band = (me % group) ^ mask
            moved = pltpu.roll(piece, (width * (band - block + group)) % LANES, 1)
            merged = jnp.where(lane_block == band, moved, merged)
        returned.append(merged)
    returned = jnp.concatenate(returned, axis=0).astype(jnp.bfloat16)
    sums = [
        lax.dot_general(returned, table_ref[pair], NT, preferred_element_type=jnp.float32)
        for pair in range(pairs_dev)
    ]
    row = lax.broadcasted_iota(jnp.int32, (1, rows_total), 1)
    degree = jnp.where(row < orders_total - lower, lower + row, row - 1).astype(jnp.float32)
    degree = degree * (degree + 1.0)
    damping = []
    for s in range(shells):
        radius = inner_radius + (s + 0.5) * shell_step
        damping.append(degree * (shell_step * shell_step / (radius * radius)))
    by_pair = at // (rows // pairs_dev)
    for f in range(fields):
        rate = factor_ref[0, f, :, 0:1]
        strength = factor_ref[1, f, :, 0:1]
        state, drive, diagonal = ([], [], [])
        for s in range(shells):
            state.append(paired_state(state_ref, f, s))
            diagonal.append(1.0 + rate * (2.0 + damping[s]))
        for s in range(shells):
            halves = []
            for h in range(2):
                start = ((h * shells + s) * fields + f) * rows
                value = sums[0][start : start + rows]
                for pair in range(1, pairs_dev):
                    value = jnp.where(by_pair == pair, sums[pair][start : start + rows], value)
                halves.append(value)
            total = halves[0] + jnp.where(odd, -halves[1], halves[1])
            total = jnp.where(member, total, 0.0)
            total = total + pltpu.roll(total, rows - 2, 0)
            laplace = state[1 - s] - 2.0 * state[s] - damping[s] * state[s]
            drive.append(state[s] + rate * (laplace + strength * total))
        factor = 1.0 / (diagonal[0] * diagonal[1] - rate * rate)
        for s in range(shells):
            updated = (diagonal[1 - s] * drive[s] + rate * drive[1 - s]) * factor
            for pair in range(pairs_dev):
                start = pair * (rows // pairs_dev)
                out_ref[pair, f, s] = updated[start : start + 2]


def banded(group, spectral_state, synthesis_table, low_orders, diffusion, coupling):
    pairs_dev, field_count, shell_count, part_count, rows_total = spectral_state.shape
    half_lat = synthesis_table.shape[2]
    orders_total = rows_total - 1
    lon_total = 3 * orders_total
    mode_count = lax.axis_size("mode")
    rows = pairs_dev * 2 * part_count
    columns = rows * mode_count
    scale = 2.0 * math.sqrt(orders_total * rows_total / (2 * half_lat * lon_total))

    def like(shape, dtype=jnp.bfloat16):
        return jax.ShapeDtypeStruct(shape, dtype)

    chunks, wave_high, wave_rest, own_waves, factors = pl.pallas_call(
        functools.partial(band_synthesis_kernel, (group, mode_count, orders_total)),
        out_shape=[
            like((columns, field_count * LANES)),
            like((lon_total, columns)),
            like((lon_total, columns)),
            like((2 * group * rows, lon_total)),
            like((2, field_count, 8, LANES), jnp.float32),
        ],
        in_specs=vmem(5),
        out_specs=vmem(5),
        compiler_params=GRANT,
        name="synthesis",
    )(low_orders, diffusion, coupling, spectral_state, synthesis_table)
    pieces = lax.all_to_all(chunks, "mode", split_axis=0, concat_axis=0, tiled=True)
    answers = pl.pallas_call(
        functools.partial(band_product_kernel, scale),
        out_shape=[like((rows, field_count * LANES))] * group,
        in_specs=vmem(4),
        out_specs=vmem(group),
        compiler_params=GRANT,
        name="products",
    )(pieces, wave_high, wave_rest, own_waves)
    returned = [answers[0]]
    for mask in range(1, group):
        ring = [(i, i ^ mask) for i in range(mode_count)]
        returned.append(lax.ppermute(answers[mask], "mode", ring))
    return pl.pallas_call(
        functools.partial(band_step_kernel, (group, orders_total)),
        out_shape=like(spectral_state.shape, jnp.float32),
        in_specs=vmem(4 + group),
        out_specs=pl.BlockSpec(memory_space=pltpu.VMEM),
        compiler_params=GRANT,
        name="step",
    )(low_orders, factors, spectral_state, synthesis_table, *returned)


def body(spectral_state, synthesis_table, low_orders, diffusion, coupling):
    radial_count = lax.axis_size("radial")
    if radial_count > 1:
        synthesis_table = lax.all_gather(synthesis_table, "radial", axis=2, tiled=True)
    pairs_dev, field_count, shell_count, part_count, rows_total = spectral_state.shape
    half_lat = synthesis_table.shape[2]
    lat_total = 2 * half_lat
    orders_total = rows_total - 1
    lon_total = 3 * orders_total
    mode_count = lax.axis_size("mode")
    chunk_rows = pairs_dev * 2 * part_count
    column_count = chunk_rows * mode_count
    count = half_lat // mode_count
    half = (field_count + 1) * shell_count
    block = 2 * half
    used = count * block
    assert half == 8 and chunk_rows * block == LANES and used <= LANES // 2 and part_count == 2
    scale = 2.0 * math.sqrt(orders_total * rows_total / (lat_total * lon_total))
    group = 2 * shell_count * half_lat // LANES
    if radial_count == 1 and shell_count == 2 and group == 4 and mode_count % group == 0:
        return banded(group, spectral_state, synthesis_table, low_orders, diffusion, coupling)
    spread = pltpu.VMEM((mode_count, chunk_rows, LANES), jnp.float32)
    sent = jax.ShapeDtypeStruct((column_count, LANES), jnp.bfloat16)
    table_shape = jax.ShapeDtypeStruct((column_count, lon_total), jnp.bfloat16)
    factor_shape = jax.ShapeDtypeStruct((2, half, LANES), jnp.float32)
    chunks, wave_high, wave_rest, factors = pl.pallas_call(
        functools.partial(synthesis_kernel, (pairs_dev, block, mode_count, orders_total)),
        out_shape=[sent, table_shape, table_shape, factor_shape],
        in_specs=vmem(5),
        out_specs=vmem(4),
        scratch_shapes=[spread],
        compiler_params=GRANT,
        name="synthesis",
    )(low_orders, diffusion, coupling, spectral_state, synthesis_table)
    pieces = lax.all_to_all(chunks, "mode", split_axis=0, concat_axis=0, tiled=True)
    answers = pl.pallas_call(
        functools.partial(product_kernel, (used, shell_count, scale)),
        out_shape=sent,
        in_specs=vmem(3),
        out_specs=pl.BlockSpec(memory_space=pltpu.VMEM),
        compiler_params=GRANT,
        name="products",
    )(pieces, wave_high, wave_rest)
    returned = lax.all_to_all(answers, "mode", split_axis=0, concat_axis=0, tiled=True)
    dims = (pairs_dev, block, count, mode_count, orders_total)
    if radial_count == 1 and shell_count == 2:
        return pl.pallas_call(
            functools.partial(step_kernel, dims),
            out_shape=jax.ShapeDtypeStruct(spectral_state.shape, jnp.float32),
            in_specs=vmem(5),
            out_specs=pl.BlockSpec(memory_space=pltpu.VMEM),
            scratch_shapes=[spread],
            compiler_params=GRANT,
            name="step",
        )(low_orders, factors, returned, synthesis_table, spectral_state)
    nonlinear = pl.pallas_call(
        functools.partial(analysis_kernel, dims),
        out_shape=jax.ShapeDtypeStruct((pairs_dev, part_count, half, rows_total), jnp.float32),
        in_specs=vmem(3),
        out_specs=pl.BlockSpec(memory_space=pltpu.VMEM),
        scratch_shapes=[spread],
        compiler_params=GRANT,
        name="analysis",
    )(low_orders, returned, synthesis_table)
    nonlinear = nonlinear.reshape(pairs_dev, part_count, field_count + 1, shell_count, rows_total)
    nonlinear = jnp.stack([nonlinear[:, :, 0], nonlinear[:, :, 2], nonlinear[:, :, 1]], axis=1)
    nonlinear = nonlinear.transpose(0, 1, 3, 2, 4)
    return solve(spectral_state, nonlinear, low_orders, diffusion, coupling)


def solve(spectral_state, nonlinear, low_orders, diffusion, coupling):
    pairs_dev, field_count, shell_count, part_count, rows_total = spectral_state.shape
    orders_total = rows_total - 1
    radial_count = lax.axis_size("radial")
    own = lax.dynamic_slice_in_dim(low_orders, lax.axis_index("mode") * pairs_dev, pairs_dev)
    row_index = lax.iota(jnp.int32, rows_total)[None, :]
    lower_col = own[:, None]
    degree = jnp.where(row_index < orders_total - lower_col, lower_col + row_index, row_index - 1)
    radial_at = lax.axis_index("radial")
    rate_col = diffusion.reshape(1, field_count, 1, 1)
    strength = coupling.reshape(1, field_count, 1, 1)
    degree_term = degree.astype(jnp.float32)
    degree_term = (degree_term * (degree_term + 1.0))[:, None, None, :] * (shell_step * shell_step)
    if radial_count > 1:
        with_edges = with_halo(spectral_state, "radial", 2, 1)
    else:
        with_edges = jnp.pad(spectral_state, ((0, 0), (0, 0), (1, 1), (0, 0), (0, 0)))
    diagonals = []
    drives = []
    for shell_at in range(shell_count):
        radius = (
            inner_radius
            + ((radial_at * shell_count + shell_at).astype(jnp.float32) + 0.5) * shell_step
        )
        damping = degree_term / (radius * radius)
        middle = with_edges[:, :, shell_at + 1]
        laplace = (
            with_edges[:, :, shell_at + 2]
            - 2.0 * middle
            + with_edges[:, :, shell_at]
            - damping * middle
        )
        drives.append(middle + rate_col * (laplace + strength * nonlinear[:, :, shell_at]))
        diagonals.append(1.0 + rate_col * (2.0 + damping))
    narrow_zero = jnp.zeros(diagonals[0].shape, jnp.float32)
    wide_zero = jnp.zeros(drives[0].shape, jnp.float32)
    pivot_prev = narrow_zero
    carry_u, carry_v, carry_w = (wide_zero, narrow_zero, narrow_zero)
    pivots, sweep_u, sweep_v, sweep_w = ([], [], [], [])
    for shell_at in range(shell_count):
        denom_at = diagonals[shell_at] + rate_col * pivot_prev
        pivot_prev = -rate_col / denom_at
        first_drive = rate_col if shell_at == 0 else 0.0
        last_drive = rate_col if shell_at == shell_count - 1 else 0.0
        carry_u = (drives[shell_at] + rate_col * carry_u) / denom_at
        carry_v = (first_drive + rate_col * carry_v) / denom_at
        carry_w = (last_drive + rate_col * carry_w) / denom_at
        pivots.append(pivot_prev)
        sweep_u.append(carry_u)
        sweep_v.append(carry_v)
        sweep_w.append(carry_w)
    solved_u, solved_v, solved_w = ([sweep_u[-1]], [sweep_v[-1]], [sweep_w[-1]])
    for shell_at in range(shell_count - 2, -1, -1):
        solved_u.insert(0, sweep_u[shell_at] - pivots[shell_at] * solved_u[0])
        solved_v.insert(0, sweep_v[shell_at] - pivots[shell_at] * solved_v[0])
        solved_w.insert(0, sweep_w[shell_at] - pivots[shell_at] * solved_w[0])
    if radial_count == 1:
        return jnp.stack(solved_u, axis=2)
    first_u, last_u = (solved_u[0], solved_u[-1])
    first_v, last_v = (solved_v[0], solved_v[-1])
    first_w, last_w = (solved_w[0], solved_w[-1])
    wide_rows = jnp.stack([first_u, last_u])[None]
    narrow_rows = jnp.stack([first_v, first_w, last_v, last_w])[None]
    wide_all, narrow_all = (
        lax.all_gather(wide_rows, "radial", axis=0, tiled=True),
        lax.all_gather(narrow_rows, "radial", axis=0, tiled=True),
    )
    chain_count = lax.axis_size("radial")
    alpha_now, beta_now = (wide_zero, narrow_zero)
    alphas, betas = ([], [])
    for member in range(chain_count):
        alphas.append(alpha_now)
        betas.append(beta_now)
        peer_first_u, peer_last_u = (wide_all[member, 0], wide_all[member, 1])
        peer_first_v, peer_first_w = (narrow_all[member, 0], narrow_all[member, 1])
        peer_last_v, peer_last_w = (narrow_all[member, 2], narrow_all[member, 3])
        shrink = 1.0 - peer_first_v * beta_now
        alpha_new = (
            peer_last_u
            - peer_last_u * peer_first_v * beta_now
            + peer_last_v * alpha_now
            + peer_last_v * peer_first_u * beta_now
        ) / shrink
        beta_new = (
            peer_last_w
            - peer_last_w * peer_first_v * beta_now
            + peer_last_v * peer_first_w * beta_now
        ) / shrink
        alpha_now, beta_now = (alpha_new, beta_new)
    next_first = wide_zero
    firsts = [None] * chain_count
    nexts = [None] * chain_count
    for member in range(chain_count - 1, -1, -1):
        nexts[member] = next_first
        peer_first_u = wide_all[member, 0]
        peer_first_v, peer_first_w = (narrow_all[member, 0], narrow_all[member, 1])
        next_first = (peer_first_u + peer_first_v * alphas[member] + peer_first_w * next_first) / (
            1.0 - peer_first_v * betas[member]
        )
        firsts[member] = next_first
    alpha_prev = lax.dynamic_index_in_dim(jnp.stack(alphas), radial_at, 0, keepdims=False)
    beta_prev = lax.dynamic_index_in_dim(jnp.stack(betas), radial_at, 0, keepdims=False)
    own_first = lax.dynamic_index_in_dim(jnp.stack(firsts), radial_at, 0, keepdims=False)
    next_first = lax.dynamic_index_in_dim(jnp.stack(nexts), radial_at, 0, keepdims=False)
    prev_last = alpha_prev + beta_prev * own_first
    outputs = []
    for shell_at in range(shell_count):
        outputs.append(
            solved_u[shell_at] + prev_last * solved_v[shell_at] + next_first * solved_w[shell_at]
        )
    return jnp.stack(outputs, axis=2)


def solution(mesh):
    placed = (P("mode", None, "radial", None, None), P("mode", None, "radial"), P(), P(), P())
    return jax.shard_map(
        body,
        mesh=mesh,
        in_specs=placed,
        out_specs=P("mode", None, "radial", None, None),
        check_vma=False,
    )
```

```python
import functools
import math

import jax
import jax.numpy as jnp
from jax import lax
from jax.experimental import pallas as pl
from jax.experimental.pallas import tpu as pltpu
from jax.sharding import PartitionSpec as P


inner_radius = 0.538
shell_step = 1.0 / 2048.0
LANES = 128
SLOT_STEP = 11
SLOT_FLIP = 29
GRANT = pltpu.CompilerParams(vmem_limit_bytes=16 * 1024 * 1024)
NT = (((1,), (1,)), ((), ()))


def with_halo(shard, axis, dim, width):
    count, length = (lax.axis_size(axis), shard.shape[dim])
    up = [(i, (i + 1) % count) for i in range(count - 1)]
    down = [(j, i) for i, j in up]
    last = lax.slice_in_dim(shard, length - width, length, axis=dim)
    first = lax.slice_in_dim(shard, 0, width, axis=dim)
    before = lax.ppermute(last, axis, up)
    after = lax.ppermute(first, axis, down)
    return jnp.concatenate([before, shard, after], axis=dim)


def own_lower(low_ref, at):
    low_row = low_ref[...][None, :]
    lane = lax.broadcasted_iota(jnp.int32, low_row.shape, 1)
    return jnp.sum(jnp.where(lane == at, low_row, 0), axis=1, keepdims=True)


def row_factors(lower, shape, orders_total):
    row = lax.broadcasted_iota(jnp.int32, shape, len(shape) - 1)
    in_lower = row < orders_total - lower
    odd_lower = lax.rem(row, 2) == 1
    odd_upper = lax.rem(row + orders_total - lower, 2) == 1
    members = (in_lower, jnp.logical_not(in_lower))
    signs = (jnp.where(odd_lower, -1.0, 1.0), jnp.where(odd_upper, -1.0, 1.0))
    return members, signs


def state_rows(state_ref, pair, part, fields):
    shells = state_ref.shape[2]
    rows = [state_ref[pair, f, s, part : part + 1, :] for f in fields for s in range(shells)]
    return jnp.concatenate(rows, axis=0)


def fill_waves(low_row, orders_total, high_ref, rest_ref, step):
    columns, lon_total = high_ref.shape
    width = lon_total // 3
    lon = lax.broadcasted_iota(jnp.int32, (step, width), 1).astype(jnp.float32)
    pair_lane = lax.broadcasted_iota(jnp.int32, (step, low_row.shape[1]), 1)
    third = math.sqrt(0.75)

    def fill(base):
        column = base + lax.broadcasted_iota(jnp.int32, (step, 1), 0)
        hit = pair_lane == column // 4
        lower = jnp.sum(jnp.where(hit, low_row, 0.0), axis=1, keepdims=True)
        is_lower = (column // 2) % 2 == 0
        is_cosine = column % 2 == 0
        order = jnp.where(is_lower, lower, orders_total - 1 - lower)
        turns = order * lon
        quad = jnp.floor(turns * (4.0 / lon_total) + 0.5)
        angle = (turns - quad * (lon_total / 4)) * (2.0 * math.pi / lon_total)
        square = angle * angle
        cosine = 1.0 + square * (
            -0.5 + square * (1.0 / 24 + square * (-1.0 / 720 + square * (1.0 / 40320)))
        )
        sine = 1.0 / 120 + square * (-1.0 / 5040 + square * (1.0 / 362880))
        sine = angle * (1.0 + square * (-1.0 / 6 + square * sine))
        quad = quad.astype(jnp.int32)
        swap = (quad & 1) == 1
        cosine, sine = (jnp.where(swap, sine, cosine), jnp.where(swap, cosine, sine))
        cosine = jnp.where(((quad + 1) & 2) == 2, -cosine, cosine)
        sine = jnp.where((quad & 2) == 2, -sine, sine)
        for at in range(3):
            turn = at * order
            turn = turn - 3.0 * jnp.floor((turn + 0.5) * (1.0 / 3.0))
            cos_at = jnp.where(turn == 0.0, 1.0, -0.5)
            sin_at = jnp.where(turn == 0.0, 0.0, jnp.where(turn == 1.0, third, -third))
            by_cosine = jnp.where(is_cosine, cos_at, -sin_at)
            by_sine = jnp.where(is_cosine, -sin_at, -cos_at)
            value = cosine * by_cosine + sine * by_sine
            high = value.astype(jnp.bfloat16)
            high_ref[pl.ds(base, step), at * width : (at + 1) * width] = high
            rest_ref[pl.ds(base, step), at * width : (at + 1) * width] = (
                value - high.astype(jnp.float32)
            ).astype(jnp.bfloat16)

    if columns <= 256:
        for base in range(0, columns, step):
            fill(base)
    else:

        @pl.loop(0, columns // step)
        def _(at):
            fill(pl.multiple_of(at * step, step))


def synthesis_kernel(
    dims,
    low_ref,
    rate_ref,
    coupling_ref,
    state_ref,
    table_ref,
    out_ref,
    high_ref,
    rest_ref,
    factor_ref,
    spread_ref,
):
    pairs_dev, block, mode_count, orders_total = dims
    fields = state_ref.shape[1]
    rows_total = state_ref.shape[-1]
    chunk_rows = out_ref.shape[0] // mode_count
    group = lax.axis_index("mode") * pairs_dev
    pieces = []
    for pair in range(pairs_dev):
        lower = own_lower(low_ref, group + pair)
        members, signs = row_factors(lower, (1, rows_total), orders_total)
        coeffs = [state_rows(state_ref, pair, part, (*range(fields), 0)) for part in range(2)]
        left = []
        for k in range(2):
            order = lower if k == 0 else orders_total - 1 - lower
            weight = jnp.where(order == 0, 1.0, 2.0)
            member = jnp.where(members[k], weight, 0.0)
            for part in range(2):
                left.append(coeffs[part] * member)
                left.append(coeffs[part] * (member * signs[k]))
        left = jnp.concatenate(left, axis=0).astype(jnp.bfloat16)
        pieces.append(jnp.dot(left, table_ref[pair], preferred_element_type=jnp.float32))
    fourier = jnp.concatenate(pieces, axis=0).astype(jnp.bfloat16).astype(jnp.float32)
    turned = fourier.T
    lane_block = lax.broadcasted_iota(jnp.int32, (mode_count, LANES), 1) // block
    count = turned.shape[0] // mode_count
    for row in range(chunk_rows):
        merged = jnp.zeros((mode_count, LANES), jnp.float32)
        for i in range(count):
            part = turned[i * mode_count : (i + 1) * mode_count]
            moved = pltpu.roll(part, (block * (i - row)) % LANES, 1)
            merged = jnp.where(lane_block == i, moved, merged)
        spread_ref[:, row, :] = merged
    out_ref[...] = spread_ref[...].reshape(out_ref.shape).astype(jnp.bfloat16)
    rows = factor_ref.shape[1]
    at = lax.broadcasted_iota(jnp.int32, (rows, LANES), 0) // (rows // (fields + 1))
    for k, ref in enumerate((rate_ref, coupling_ref)):
        values = ref[...][None, :]
        factor = jnp.broadcast_to(values[:, 0:1], (rows, LANES))
        factor = jnp.where(at == 1, values[:, 2:3], factor)
        factor_ref[k] = jnp.where(at == 2, values[:, 1:2], factor)
    fill_waves(low_ref[...][None, :].astype(jnp.float32), orders_total, high_ref, rest_ref, 32)


def product_kernel(dims, sent_ref, high_ref, rest_ref, out_ref):
    used, shells, scale = dims
    turned = sent_ref[...].astype(jnp.float32).T[:used].astype(jnp.bfloat16)
    grid = jnp.dot(turned, high_ref[...], preferred_element_type=jnp.float32)
    grid = grid + jnp.dot(turned, rest_ref[...], preferred_element_type=jnp.float32)
    products = grid * pltpu.roll(grid, used - shells, 0)
    high = products.astype(jnp.bfloat16)
    rest = (products - high.astype(jnp.float32)).astype(jnp.bfloat16)
    both = lax.dot_general(
        high_ref[...], jnp.concatenate([high, rest], axis=0), NT, preferred_element_type=jnp.float32
    )
    totals = lax.dot_general(rest_ref[...], high, NT, preferred_element_type=jnp.float32)
    totals = totals + both[:, :used] + both[:, used:]
    answers = (totals * scale).astype(jnp.bfloat16)
    out_ref[...] = jnp.concatenate(
        [answers, jnp.zeros((answers.shape[0], LANES - used), jnp.bfloat16)], axis=1
    )


def analysis_sums(dims, low_ref, sent_ref, table_ref, spread_ref, emit):
    pairs_dev, block, count, mode_count, orders_total = dims
    rows_total = table_ref.shape[1]
    chunk_rows = sent_ref.shape[0] // mode_count
    group = lax.axis_index("mode") * pairs_dev
    spread_ref[...] = sent_ref[...].astype(jnp.float32).reshape(spread_ref.shape)
    lane_block = lax.broadcasted_iota(jnp.int32, (mode_count, LANES), 1) // block
    parts = [jnp.zeros((mode_count, LANES), jnp.float32) for _ in range(count)]
    for row in range(chunk_rows):
        piece = spread_ref[:, row, :]
        for i in range(count):
            moved = pltpu.roll(piece, (block * (row - i)) % LANES, 1)
            parts[i] = jnp.where(lane_block == row, moved, parts[i])
    returned = jnp.concatenate(parts, axis=0).T.astype(jnp.bfloat16)
    per_pair = returned.shape[0] // pairs_dev
    half = block // 2
    for pair in range(pairs_dev):
        lower = own_lower(low_ref, group + pair)
        members, signs = row_factors(lower, (1, rows_total), orders_total)
        sums = lax.dot_general(
            returned[pair * per_pair : (pair + 1) * per_pair],
            table_ref[pair],
            NT,
            preferred_element_type=jnp.float32,
        )
        for part in range(2):
            total = jnp.zeros((half, rows_total), jnp.float32)
            for k in range(2):
                at = (k * 2 + part) * block
                north = sums[at : at + half]
                south = sums[at + half : at + block]
                total = jnp.where(members[k], north + signs[k] * south, total)
            emit(pair, part, lower, total)


def analysis_kernel(dims, low_ref, sent_ref, table_ref, out_ref, spread_ref):
    def emit(pair, part, lower, total):
        out_ref[pair, part] = total

    analysis_sums(dims, low_ref, sent_ref, table_ref, spread_ref, emit)


def step_kernel(
    dims, low_ref, factor_ref, sent_ref, table_ref, state_ref, out_ref, spread_ref
):
    orders_total = dims[-1]
    rows_total = table_ref.shape[1]
    half = dims[1] // 2
    fields = (0, 2, 1, 0)
    at = lax.broadcasted_iota(jnp.int32, (half, 1), 0)
    upper = at % 2 == 1

    def other(value):
        return jnp.where(upper, pltpu.roll(value, 1, 0), pltpu.roll(value, half - 1, 0))

    rate = factor_ref[0, :, 0:1]
    strength = factor_ref[1, :, 0:1]
    radius = inner_radius + (jnp.where(upper, 1.0, 0.0) + 0.5) * shell_step
    inverse = (shell_step * shell_step) / (radius * radius)
    row = lax.broadcasted_iota(jnp.int32, (1, rows_total), 1)
    cache = {}

    def emit(pair, part, lower, total):
        if pair not in cache:
            degree = jnp.where(row < orders_total - lower, lower + row, row - 1).astype(jnp.float32)
            damping = (degree * (degree + 1.0)) * inverse
            diagonal = 1.0 + rate * (2.0 + damping)
            crossed = other(diagonal)
            factor = 1.0 / (diagonal * crossed - rate * rate)
            cache[pair] = (damping, crossed * factor, rate * factor)
        damping, own, across = cache[pair]
        state = state_rows(state_ref, pair, part, fields)
        laplace = other(state) - 2.0 * state - damping * state
        drive = state + rate * (laplace + strength * total)
        updated = own * drive + across * other(drive)
        for k, f in enumerate(fields[:3]):
            for s in range(2):
                out_ref[pair, f, s, part : part + 1, :] = updated[2 * k + s : 2 * k + s + 1]

    analysis_sums(dims, low_ref, sent_ref, table_ref, spread_ref, emit)


def vmem(count):
    return [pl.BlockSpec(memory_space=pltpu.VMEM)] * count


def row_lower(low_ref, first, rows, pairs_dev):
    at = lax.broadcasted_iota(jnp.int32, (rows, 1), 0)
    lower = jnp.zeros((rows, 1), jnp.int32)
    for pair in range(pairs_dev):
        lower = jnp.where(at // (rows // pairs_dev) == pair, own_lower(low_ref, first + pair), lower)
    return at, lower


def row_members(at, lower, rows_total, orders_total):
    row = lax.broadcasted_iota(jnp.int32, (1, rows_total), 1)
    upper = (at // 2) % 2 == 1
    edge = orders_total - lower
    member = jnp.logical_xor(row < edge, upper)
    odd = ((row + jnp.where(upper, edge, 0)) & 1) == 1
    return member, odd


def paired_state(state_ref, field, shell):
    pairs_dev = state_ref.shape[0]
    pieces = [state_ref[pair, field, shell] for pair in range(pairs_dev) for _ in range(2)]
    return jnp.concatenate(pieces, axis=0)


def wave_values(turns, lon_total):
    quad = jnp.floor(turns * (4.0 / lon_total) + 0.5)
    angle = (turns - quad * (lon_total / 4)) * (2.0 * math.pi / lon_total)
    square = angle * angle
    cosine = 1.0 + square * (
        -0.5 + square * (1.0 / 24 + square * (-1.0 / 720 + square * (1.0 / 40320)))
    )
    sine = 1.0 / 120 + square * (-1.0 / 5040 + square * (1.0 / 362880))
    sine = angle * (1.0 + square * (-1.0 / 6 + square * sine))
    quad = quad.astype(jnp.int32)
    swap = (quad & 1) == 1
    cosine, sine = (jnp.where(swap, sine, cosine), jnp.where(swap, cosine, sine))
    cosine = jnp.where(((quad + 1) & 2) == 2, -cosine, cosine)
    sine = jnp.where((quad & 2) == 2, -sine, sine)
    return cosine, sine


def third_factors(order, is_cosine, at):
    third = math.sqrt(0.75)
    turn = at * order
    turn = turn - 3.0 * jnp.floor((turn + 0.5) * (1.0 / 3.0))
    cos_at = jnp.where(turn == 0.0, 1.0, -0.5)
    sin_at = jnp.where(turn == 0.0, 0.0, jnp.where(turn == 1.0, third, -third))
    by_cosine = jnp.where(is_cosine, cos_at, -sin_at)
    by_sine = jnp.where(is_cosine, -sin_at, -cos_at)
    return by_cosine, by_sine


def two_terms(value):
    high = value.astype(jnp.bfloat16)
    return high, (value - high.astype(jnp.float32)).astype(jnp.bfloat16)


def slot_device(slot, mode_count):
    return ((SLOT_STEP * slot) ^ SLOT_FLIP) & (mode_count - 1)


def band_of(device, mode_count):
    return (device & 1) | (((device // (mode_count // 4)) & 1) << 1)


def member_step(mask, mode_count):
    return (mask & 1) | ((mask >> 1) * (mode_count // 4))


def band_synthesis_kernel(
    dims,
    low_ref,
    rate_ref,
    coupling_ref,
    state_ref,
    table_ref,
    out_ref,
    high_ref,
    rest_ref,
    own_ref,
    factor_ref,
):
    group, mode_count, orders_total = dims
    pairs_dev, fields, shells, _, rows_total = state_ref.shape
    rows = out_ref.shape[0] // mode_count
    me = lax.axis_index("mode")
    at, lower = row_lower(low_ref, me * pairs_dev, rows, pairs_dev)
    member, odd = row_members(at, lower, rows_total, orders_total)
    order = jnp.where((at // 2) % 2 == 1, orders_total - 1 - lower, lower)
    weight = jnp.where(order == 0, 1.0, 2.0)
    north = jnp.where(member, weight, 0.0)
    south = jnp.where(odd, -north, north)
    state = [[paired_state(state_ref, f, s) for f in range(fields)] for s in range(shells)]
    fourier = None
    for pair in range(pairs_dev):
        mine = at // (rows // pairs_dev) == pair
        left = [
            state[s][f] * jnp.where(mine, factor, 0.0)
            for factor in (north, south)
            for s in range(shells)
            for f in range(fields)
        ]
        left = jnp.concatenate(left, axis=0).astype(jnp.bfloat16)
        part = jnp.dot(left, table_ref[pair], preferred_element_type=jnp.float32)
        fourier = part if fourier is None else fourier + part
    fourier = fourier.astype(jnp.bfloat16).astype(jnp.float32)
    width = LANES // group
    lane_block = lax.broadcasted_iota(jnp.int32, (fields * rows, LANES), 1) // width
    for band in range(group):
        piece = None
        for block in range(group):
            source = fourier[block * fields * rows : (block + 1) * fields * rows]
            moved = pltpu.roll(source, (width * (block - band)) % LANES, 1)
            piece = moved if piece is None else jnp.where(lane_block == block, moved, piece)
        for field in range(fields):
            value = piece[field * rows : (field + 1) * rows].astype(jnp.bfloat16)
            for slot in range(mode_count):
                if band_of(slot_device(slot, mode_count), mode_count) == band:
                    out_ref[slot * rows : (slot + 1) * rows, field * LANES : (field + 1) * LANES] = value

    lon_total, columns = high_ref.shape
    span = lon_total // 3
    low_row = low_ref[...][None, :].astype(jnp.float32)
    pair_at = lax.broadcasted_iota(jnp.int32, (low_row.shape[1], columns), 0)
    column = lax.broadcasted_iota(jnp.int32, (low_row.shape[1], columns), 1)
    device = slot_device(column // rows, mode_count)
    spread = jnp.where(device * pairs_dev + (column % rows) // 4 == pair_at, 1.0, 0.0).astype(jnp.bfloat16)
    lowers = jnp.broadcast_to(low_row, (8, low_row.shape[1])).astype(jnp.bfloat16)
    lowers = jnp.dot(lowers, spread, preferred_element_type=jnp.float32)[0:1]
    column = lax.broadcasted_iota(jnp.int32, (1, columns), 1)
    orders = jnp.where((column // 2) % 2 == 0, lowers, orders_total - 1 - lowers)
    is_cosine = column % 2 == 0
    factors = [third_factors(orders, is_cosine, third) for third in range(3)]
    step = min(span, 32)
    for base in range(0, span, step):
        lon = (base + lax.broadcasted_iota(jnp.int32, (step, 1), 0)).astype(jnp.float32)
        cosine, sine = wave_values(lon * orders, lon_total)
        for third, (by_cosine, by_sine) in enumerate(factors):
            high, rest = two_terms(cosine * by_cosine + sine * by_sine)
            high_ref[third * span + base : third * span + base + step, :] = high
            rest_ref[third * span + base : third * span + base + step, :] = rest
    count = group * rows
    at = lax.broadcasted_iota(jnp.int32, (count, 1), 0)
    device = me ^ member_step(at // rows, mode_count)
    pair_index = device * pairs_dev + (at % rows) // 4
    pair_lane = lax.broadcasted_iota(jnp.int32, (count, low_row.shape[1]), 1)
    lowers = jnp.sum(jnp.where(pair_lane == pair_index, low_row, 0.0), axis=1, keepdims=True)
    orders = jnp.where((at // 2) % 2 == 0, lowers, orders_total - 1 - lowers)
    is_cosine = at % 2 == 0
    lon = lax.broadcasted_iota(jnp.int32, (1, span), 1).astype(jnp.float32)
    cosine, sine = wave_values(lon * orders, lon_total)
    for third in range(3):
        by_cosine, by_sine = third_factors(orders, is_cosine, third)
        high, rest = two_terms(cosine * by_cosine + sine * by_sine)
        own_ref[:count, third * span : (third + 1) * span] = high
        own_ref[count:, third * span : (third + 1) * span] = rest
    for k, ref in enumerate((rate_ref, coupling_ref)):
        for f in range(fields):
            factor_ref[k, f] = jnp.broadcast_to(ref[...][None, f : f + 1], (8, LANES))


def band_product_kernel(scale, sent_ref, high_ref, rest_ref, own_ref, *out_refs):
    sent = sent_ref[...]
    grid = jnp.dot(high_ref[...], sent, preferred_element_type=jnp.float32)
    grid = grid + jnp.dot(rest_ref[...], sent, preferred_element_type=jnp.float32)
    width = sent.shape[1] // 3
    first, second, third = (grid[:, f * width : (f + 1) * width] for f in range(3))
    products = jnp.concatenate([first * second, first * third, second * third], axis=1)
    high, rest = two_terms(products)
    count = own_ref.shape[0] // 2
    both = jnp.dot(own_ref[...], high, preferred_element_type=jnp.float32)
    totals = jnp.dot(own_ref[:count], rest, preferred_element_type=jnp.float32)
    totals = totals + both[:count] + both[count:]
    answers = (totals * scale).astype(jnp.bfloat16)
    rows = count // len(out_refs)
    for at, out_ref in enumerate(out_refs):
        out_ref[...] = answers[at * rows : (at + 1) * rows]


def band_step_kernel(dims, low_ref, factor_ref, state_ref, table_ref, *refs):
    group, mode_count, orders_total = dims
    sent_refs, out_ref = (refs[:group], refs[group])
    pairs_dev, fields, shells, _, rows_total = state_ref.shape
    rows = sent_refs[0].shape[0]
    me = lax.axis_index("mode")
    at, lower = row_lower(low_ref, me * pairs_dev, rows, pairs_dev)
    member, odd = row_members(at, lower, rows_total, orders_total)
    width = LANES // group
    lane_block = lax.broadcasted_iota(jnp.int32, (fields * rows, LANES), 1) // width
    pieces = []
    for ref in sent_refs:
        value = ref[...].astype(jnp.float32)
        pieces.append(
            jnp.concatenate([value[:, f * LANES : (f + 1) * LANES] for f in range(fields)], axis=0)
        )
    returned = []
    for block in range(group):
        merged = jnp.zeros((fields * rows, LANES), jnp.float32)
        for mask, piece in enumerate(pieces):
            band = band_of(me, mode_count) ^ mask
            moved = pltpu.roll(piece, (width * (band - block + group)) % LANES, 1)
            merged = jnp.where(lane_block == band, moved, merged)
        returned.append(merged)
    returned = jnp.concatenate(returned, axis=0).astype(jnp.bfloat16)
    sums = [
        lax.dot_general(returned, table_ref[pair], NT, preferred_element_type=jnp.float32)
        for pair in range(pairs_dev)
    ]
    row = lax.broadcasted_iota(jnp.int32, (1, rows_total), 1)
    degree = jnp.where(row < orders_total - lower, lower + row, row - 1).astype(jnp.float32)
    degree = degree * (degree + 1.0)
    damping = []
    for s in range(shells):
        radius = inner_radius + (s + 0.5) * shell_step
        damping.append(degree * (shell_step * shell_step / (radius * radius)))
    by_pair = at // (rows // pairs_dev)
    for f in range(fields):
        rate = factor_ref[0, f, :, 0:1]
        strength = factor_ref[1, f, :, 0:1]
        state, drive, diagonal = ([], [], [])
        for s in range(shells):
            state.append(paired_state(state_ref, f, s))
            diagonal.append(1.0 + rate * (2.0 + damping[s]))
        for s in range(shells):
            halves = []
            for h in range(2):
                start = ((h * shells + s) * fields + f) * rows
                value = sums[0][start : start + rows]
                for pair in range(1, pairs_dev):
                    value = jnp.where(by_pair == pair, sums[pair][start : start + rows], value)
                halves.append(value)
            total = halves[0] + jnp.where(odd, -halves[1], halves[1])
            total = jnp.where(member, total, 0.0)
            total = total + pltpu.roll(total, rows - 2, 0)
            laplace = state[1 - s] - 2.0 * state[s] - damping[s] * state[s]
            drive.append(state[s] + rate * (laplace + strength * total))
        factor = 1.0 / (diagonal[0] * diagonal[1] - rate * rate)
        for s in range(shells):
            updated = (diagonal[1 - s] * drive[s] + rate * drive[1 - s]) * factor
            for pair in range(pairs_dev):
                start = pair * (rows // pairs_dev)
                out_ref[pair, f, s] = updated[start : start + 2]


def banded(group, spectral_state, synthesis_table, low_orders, diffusion, coupling):
    pairs_dev, field_count, _, part_count, rows_total = spectral_state.shape
    half_lat = synthesis_table.shape[2]
    orders_total = rows_total - 1
    lon_total = 3 * orders_total
    mode_count = lax.axis_size("mode")
    rows = pairs_dev * 2 * part_count
    columns = rows * mode_count
    scale = 2.0 * math.sqrt(orders_total * rows_total / (2 * half_lat * lon_total))

    def like(shape, dtype=jnp.bfloat16):
        return jax.ShapeDtypeStruct(shape, dtype)

    chunks, wave_high, wave_rest, own_waves, factors = pl.pallas_call(
        functools.partial(band_synthesis_kernel, (group, mode_count, orders_total)),
        out_shape=[
            like((columns, field_count * LANES)),
            like((lon_total, columns)),
            like((lon_total, columns)),
            like((2 * group * rows, lon_total)),
            like((2, field_count, 8, LANES), jnp.float32),
        ],
        in_specs=vmem(5),
        out_specs=vmem(5),
        compiler_params=GRANT,
        name="synthesis",
    )(low_orders, diffusion, coupling, spectral_state, synthesis_table)
    slots = [slot_device(slot, mode_count) for slot in range(mode_count)]
    pieces = lax.all_to_all(
        chunks, "mode", split_axis=0, concat_axis=0, tiled=True, axis_index_groups=[slots]
    )
    answers = pl.pallas_call(
        functools.partial(band_product_kernel, scale),
        out_shape=[like((rows, field_count * LANES))] * group,
        in_specs=vmem(4),
        out_specs=vmem(group),
        compiler_params=GRANT,
        name="products",
    )(pieces, wave_high, wave_rest, own_waves)
    returned = [answers[0]]
    for mask in range(1, group):
        ring = [(i, i ^ member_step(mask, mode_count)) for i in range(mode_count)]
        returned.append(lax.ppermute(answers[mask], "mode", ring))
    return pl.pallas_call(
        functools.partial(band_step_kernel, (group, mode_count, orders_total)),
        out_shape=like(spectral_state.shape, jnp.float32),
        in_specs=vmem(4 + group),
        out_specs=pl.BlockSpec(memory_space=pltpu.VMEM),
        compiler_params=GRANT,
        name="step",
    )(low_orders, factors, spectral_state, synthesis_table, *returned)


def body(spectral_state, synthesis_table, low_orders, diffusion, coupling):
    radial_count = lax.axis_size("radial")
    if radial_count > 1:
        synthesis_table = lax.all_gather(synthesis_table, "radial", axis=2, tiled=True)
    pairs_dev, field_count, shell_count, part_count, rows_total = spectral_state.shape
    half_lat = synthesis_table.shape[2]
    lat_total = 2 * half_lat
    orders_total = rows_total - 1
    lon_total = 3 * orders_total
    mode_count = lax.axis_size("mode")
    chunk_rows = pairs_dev * 2 * part_count
    column_count = chunk_rows * mode_count
    count = half_lat // mode_count
    half = (field_count + 1) * shell_count
    block = 2 * half
    used = count * block
    assert half == 8 and chunk_rows * block == LANES and used <= LANES // 2 and part_count == 2
    scale = 2.0 * math.sqrt(orders_total * rows_total / (lat_total * lon_total))
    group = 2 * shell_count * half_lat // LANES
    if radial_count == 1 and shell_count == 2 and group == 4 and mode_count >= 8 and mode_count & (mode_count - 1) == 0:
        return banded(group, spectral_state, synthesis_table, low_orders, diffusion, coupling)
    spread = pltpu.VMEM((mode_count, chunk_rows, LANES), jnp.float32)
    sent = jax.ShapeDtypeStruct((column_count, LANES), jnp.bfloat16)
    table_shape = jax.ShapeDtypeStruct((column_count, lon_total), jnp.bfloat16)
    factor_shape = jax.ShapeDtypeStruct((2, half, LANES), jnp.float32)
    chunks, wave_high, wave_rest, factors = pl.pallas_call(
        functools.partial(synthesis_kernel, (pairs_dev, block, mode_count, orders_total)),
        out_shape=[sent, table_shape, table_shape, factor_shape],
        in_specs=vmem(5),
        out_specs=vmem(4),
        scratch_shapes=[spread],
        compiler_params=GRANT,
        name="synthesis",
    )(low_orders, diffusion, coupling, spectral_state, synthesis_table)
    pieces = lax.all_to_all(chunks, "mode", split_axis=0, concat_axis=0, tiled=True)
    answers = pl.pallas_call(
        functools.partial(product_kernel, (used, shell_count, scale)),
        out_shape=sent,
        in_specs=vmem(3),
        out_specs=pl.BlockSpec(memory_space=pltpu.VMEM),
        compiler_params=GRANT,
        name="products",
    )(pieces, wave_high, wave_rest)
    returned = lax.all_to_all(answers, "mode", split_axis=0, concat_axis=0, tiled=True)
    dims = (pairs_dev, block, count, mode_count, orders_total)
    if radial_count == 1 and shell_count == 2:
        return pl.pallas_call(
            functools.partial(step_kernel, dims),
            out_shape=jax.ShapeDtypeStruct(spectral_state.shape, jnp.float32),
            in_specs=vmem(5),
            out_specs=pl.BlockSpec(memory_space=pltpu.VMEM),
            scratch_shapes=[spread],
            compiler_params=GRANT,
            name="step",
        )(low_orders, factors, returned, synthesis_table, spectral_state)
    nonlinear = pl.pallas_call(
        functools.partial(analysis_kernel, dims),
        out_shape=jax.ShapeDtypeStruct((pairs_dev, part_count, half, rows_total), jnp.float32),
        in_specs=vmem(3),
        out_specs=pl.BlockSpec(memory_space=pltpu.VMEM),
        scratch_shapes=[spread],
        compiler_params=GRANT,
        name="analysis",
    )(low_orders, returned, synthesis_table)
    nonlinear = nonlinear.reshape(pairs_dev, part_count, field_count + 1, shell_count, rows_total)
    nonlinear = jnp.stack([nonlinear[:, :, 0], nonlinear[:, :, 2], nonlinear[:, :, 1]], axis=1)
    nonlinear = nonlinear.transpose(0, 1, 3, 2, 4)
    return solve(spectral_state, nonlinear, low_orders, diffusion, coupling)


def solve(spectral_state, nonlinear, low_orders, diffusion, coupling):
    pairs_dev, field_count, shell_count, _, rows_total = spectral_state.shape
    orders_total = rows_total - 1
    radial_count = lax.axis_size("radial")
    own = lax.dynamic_slice_in_dim(low_orders, lax.axis_index("mode") * pairs_dev, pairs_dev)
    row_index = lax.iota(jnp.int32, rows_total)[None, :]
    lower_col = own[:, None]
    degree = jnp.where(row_index < orders_total - lower_col, lower_col + row_index, row_index - 1)
    radial_at = lax.axis_index("radial")
    rate_col = diffusion.reshape(1, field_count, 1, 1)
    strength = coupling.reshape(1, field_count, 1, 1)
    degree_term = degree.astype(jnp.float32)
    degree_term = (degree_term * (degree_term + 1.0))[:, None, None, :] * (shell_step * shell_step)
    if radial_count > 1:
        with_edges = with_halo(spectral_state, "radial", 2, 1)
    else:
        with_edges = jnp.pad(spectral_state, ((0, 0), (0, 0), (1, 1), (0, 0), (0, 0)))
    diagonals = []
    drives = []
    for shell_at in range(shell_count):
        radius = (
            inner_radius
            + ((radial_at * shell_count + shell_at).astype(jnp.float32) + 0.5) * shell_step
        )
        damping = degree_term / (radius * radius)
        middle = with_edges[:, :, shell_at + 1]
        laplace = (
            with_edges[:, :, shell_at + 2]
            - 2.0 * middle
            + with_edges[:, :, shell_at]
            - damping * middle
        )
        drives.append(middle + rate_col * (laplace + strength * nonlinear[:, :, shell_at]))
        diagonals.append(1.0 + rate_col * (2.0 + damping))
    narrow_zero = jnp.zeros(diagonals[0].shape, jnp.float32)
    wide_zero = jnp.zeros(drives[0].shape, jnp.float32)
    pivot_prev = narrow_zero
    carry_u, carry_v, carry_w = (wide_zero, narrow_zero, narrow_zero)
    pivots, sweep_u, sweep_v, sweep_w = ([], [], [], [])
    for shell_at in range(shell_count):
        denom_at = diagonals[shell_at] + rate_col * pivot_prev
        pivot_prev = -rate_col / denom_at
        first_drive = rate_col if shell_at == 0 else 0.0
        last_drive = rate_col if shell_at == shell_count - 1 else 0.0
        carry_u = (drives[shell_at] + rate_col * carry_u) / denom_at
        carry_v = (first_drive + rate_col * carry_v) / denom_at
        carry_w = (last_drive + rate_col * carry_w) / denom_at
        pivots.append(pivot_prev)
        sweep_u.append(carry_u)
        sweep_v.append(carry_v)
        sweep_w.append(carry_w)
    solved_u, solved_v, solved_w = ([sweep_u[-1]], [sweep_v[-1]], [sweep_w[-1]])
    for shell_at in range(shell_count - 2, -1, -1):
        solved_u.insert(0, sweep_u[shell_at] - pivots[shell_at] * solved_u[0])
        solved_v.insert(0, sweep_v[shell_at] - pivots[shell_at] * solved_v[0])
        solved_w.insert(0, sweep_w[shell_at] - pivots[shell_at] * solved_w[0])
    if radial_count == 1:
        return jnp.stack(solved_u, axis=2)
    first_u, last_u = (solved_u[0], solved_u[-1])
    first_v, last_v = (solved_v[0], solved_v[-1])
    first_w, last_w = (solved_w[0], solved_w[-1])
    wide_rows = jnp.stack([first_u, last_u])[None]
    narrow_rows = jnp.stack([first_v, first_w, last_v, last_w])[None]
    wide_all, narrow_all = (
        lax.all_gather(wide_rows, "radial", axis=0, tiled=True),
        lax.all_gather(narrow_rows, "radial", axis=0, tiled=True),
    )
    chain_count = lax.axis_size("radial")
    alpha_now, beta_now = (wide_zero, narrow_zero)
    alphas, betas = ([], [])
    for member in range(chain_count):
        alphas.append(alpha_now)
        betas.append(beta_now)
        peer_first_u, peer_last_u = (wide_all[member, 0], wide_all[member, 1])
        peer_first_v, peer_first_w = (narrow_all[member, 0], narrow_all[member, 1])
        peer_last_v, peer_last_w = (narrow_all[member, 2], narrow_all[member, 3])
        shrink = 1.0 - peer_first_v * beta_now
        alpha_new = (
            peer_last_u
            - peer_last_u * peer_first_v * beta_now
            + peer_last_v * alpha_now
            + peer_last_v * peer_first_u * beta_now
        ) / shrink
        beta_new = (
            peer_last_w
            - peer_last_w * peer_first_v * beta_now
            + peer_last_v * peer_first_w * beta_now
        ) / shrink
        alpha_now, beta_now = (alpha_new, beta_new)
    next_first = wide_zero
    firsts = [None] * chain_count
    nexts = [None] * chain_count
    for member in range(chain_count - 1, -1, -1):
        nexts[member] = next_first
        peer_first_u = wide_all[member, 0]
        peer_first_v, peer_first_w = (narrow_all[member, 0], narrow_all[member, 1])
        next_first = (peer_first_u + peer_first_v * alphas[member] + peer_first_w * next_first) / (
            1.0 - peer_first_v * betas[member]
        )
        firsts[member] = next_first
    alpha_prev = lax.dynamic_index_in_dim(jnp.stack(alphas), radial_at, 0, keepdims=False)
    beta_prev = lax.dynamic_index_in_dim(jnp.stack(betas), radial_at, 0, keepdims=False)
    own_first = lax.dynamic_index_in_dim(jnp.stack(firsts), radial_at, 0, keepdims=False)
    next_first = lax.dynamic_index_in_dim(jnp.stack(nexts), radial_at, 0, keepdims=False)
    prev_last = alpha_prev + beta_prev * own_first
    outputs = []
    for shell_at in range(shell_count):
        outputs.append(
            solved_u[shell_at] + prev_last * solved_v[shell_at] + next_first * solved_w[shell_at]
        )
    return jnp.stack(outputs, axis=2)


def solution(mesh):
    placed = (P("mode", None, "radial", None, None), P("mode", None, "radial"), P(), P(), P())
    return jax.shard_map(
        body,
        mesh=mesh,
        in_specs=placed,
        out_specs=P("mode", None, "radial", None, None),
        check_vma=False,
    )
```

```python
import functools
import math

import jax
import jax.numpy as jnp
from jax import lax
from jax.experimental import pallas as pl
from jax.experimental.pallas import tpu as pltpu
from jax.sharding import PartitionSpec as P


inner_radius = 0.538
shell_step = 1.0 / 2048.0
LANES = 128
SLOT_STEP = 11
SLOT_FLIP = 29
GRANT = pltpu.CompilerParams(vmem_limit_bytes=16 * 1024 * 1024)
NT = (((1,), (1,)), ((), ()))


def with_halo(shard, axis, dim, width):
    count, length = (lax.axis_size(axis), shard.shape[dim])
    up = [(i, (i + 1) % count) for i in range(count - 1)]
    down = [(j, i) for i, j in up]
    last = lax.slice_in_dim(shard, length - width, length, axis=dim)
    first = lax.slice_in_dim(shard, 0, width, axis=dim)
    before = lax.ppermute(last, axis, up)
    after = lax.ppermute(first, axis, down)
    return jnp.concatenate([before, shard, after], axis=dim)


def own_lower(low_ref, at):
    low_row = low_ref[...][None, :]
    lane = lax.broadcasted_iota(jnp.int32, low_row.shape, 1)
    return jnp.sum(jnp.where(lane == at, low_row, 0), axis=1, keepdims=True)


def row_factors(lower, shape, orders_total):
    row = lax.broadcasted_iota(jnp.int32, shape, len(shape) - 1)
    in_lower = row < orders_total - lower
    odd_lower = lax.rem(row, 2) == 1
    odd_upper = lax.rem(row + orders_total - lower, 2) == 1
    members = (in_lower, jnp.logical_not(in_lower))
    signs = (jnp.where(odd_lower, -1.0, 1.0), jnp.where(odd_upper, -1.0, 1.0))
    return members, signs


def state_rows(state_ref, pair, part, fields):
    shells = state_ref.shape[2]
    rows = [state_ref[pair, f, s, part : part + 1, :] for f in fields for s in range(shells)]
    return jnp.concatenate(rows, axis=0)


def fill_waves(low_row, orders_total, high_ref, rest_ref, step):
    columns, lon_total = high_ref.shape
    width = lon_total // 3
    lon = lax.broadcasted_iota(jnp.int32, (step, width), 1).astype(jnp.float32)
    pair_lane = lax.broadcasted_iota(jnp.int32, (step, low_row.shape[1]), 1)
    third = math.sqrt(0.75)

    def fill(base):
        column = base + lax.broadcasted_iota(jnp.int32, (step, 1), 0)
        hit = pair_lane == column // 4
        lower = jnp.sum(jnp.where(hit, low_row, 0.0), axis=1, keepdims=True)
        is_lower = (column // 2) % 2 == 0
        is_cosine = column % 2 == 0
        order = jnp.where(is_lower, lower, orders_total - 1 - lower)
        turns = order * lon
        quad = jnp.floor(turns * (4.0 / lon_total) + 0.5)
        angle = (turns - quad * (lon_total / 4)) * (2.0 * math.pi / lon_total)
        square = angle * angle
        cosine = 1.0 + square * (
            -0.5 + square * (1.0 / 24 + square * (-1.0 / 720 + square * (1.0 / 40320)))
        )
        sine = 1.0 / 120 + square * (-1.0 / 5040 + square * (1.0 / 362880))
        sine = angle * (1.0 + square * (-1.0 / 6 + square * sine))
        quad = quad.astype(jnp.int32)
        swap = (quad & 1) == 1
        cosine, sine = (jnp.where(swap, sine, cosine), jnp.where(swap, cosine, sine))
        cosine = jnp.where(((quad + 1) & 2) == 2, -cosine, cosine)
        sine = jnp.where((quad & 2) == 2, -sine, sine)
        for at in range(3):
            turn = at * order
            turn = turn - 3.0 * jnp.floor((turn + 0.5) * (1.0 / 3.0))
            cos_at = jnp.where(turn == 0.0, 1.0, -0.5)
            sin_at = jnp.where(turn == 0.0, 0.0, jnp.where(turn == 1.0, third, -third))
            by_cosine = jnp.where(is_cosine, cos_at, -sin_at)
            by_sine = jnp.where(is_cosine, -sin_at, -cos_at)
            value = cosine * by_cosine + sine * by_sine
            high = value.astype(jnp.bfloat16)
            high_ref[pl.ds(base, step), at * width : (at + 1) * width] = high
            rest_ref[pl.ds(base, step), at * width : (at + 1) * width] = (
                value - high.astype(jnp.float32)
            ).astype(jnp.bfloat16)

    if columns <= 256:
        for base in range(0, columns, step):
            fill(base)
    else:

        @pl.loop(0, columns // step)
        def _(at):
            fill(pl.multiple_of(at * step, step))


def synthesis_kernel(
    dims,
    low_ref,
    rate_ref,
    coupling_ref,
    state_ref,
    table_ref,
    out_ref,
    high_ref,
    rest_ref,
    factor_ref,
    spread_ref,
):
    pairs_dev, block, mode_count, orders_total = dims
    fields = state_ref.shape[1]
    rows_total = state_ref.shape[-1]
    chunk_rows = out_ref.shape[0] // mode_count
    group = lax.axis_index("mode") * pairs_dev
    pieces = []
    for pair in range(pairs_dev):
        lower = own_lower(low_ref, group + pair)
        members, signs = row_factors(lower, (1, rows_total), orders_total)
        coeffs = [state_rows(state_ref, pair, part, (*range(fields), 0)) for part in range(2)]
        left = []
        for k in range(2):
            order = lower if k == 0 else orders_total - 1 - lower
            weight = jnp.where(order == 0, 1.0, 2.0)
            member = jnp.where(members[k], weight, 0.0)
            for part in range(2):
                left.append(coeffs[part] * member)
                left.append(coeffs[part] * (member * signs[k]))
        left = jnp.concatenate(left, axis=0).astype(jnp.bfloat16)
        pieces.append(jnp.dot(left, table_ref[pair], preferred_element_type=jnp.float32))
    fourier = jnp.concatenate(pieces, axis=0).astype(jnp.bfloat16).astype(jnp.float32)
    turned = fourier.T
    lane_block = lax.broadcasted_iota(jnp.int32, (mode_count, LANES), 1) // block
    count = turned.shape[0] // mode_count
    for row in range(chunk_rows):
        merged = jnp.zeros((mode_count, LANES), jnp.float32)
        for i in range(count):
            part = turned[i * mode_count : (i + 1) * mode_count]
            moved = pltpu.roll(part, (block * (i - row)) % LANES, 1)
            merged = jnp.where(lane_block == i, moved, merged)
        spread_ref[:, row, :] = merged
    out_ref[...] = spread_ref[...].reshape(out_ref.shape).astype(jnp.bfloat16)
    rows = factor_ref.shape[1]
    at = lax.broadcasted_iota(jnp.int32, (rows, LANES), 0) // (rows // (fields + 1))
    for k, ref in enumerate((rate_ref, coupling_ref)):
        values = ref[...][None, :]
        factor = jnp.broadcast_to(values[:, 0:1], (rows, LANES))
        factor = jnp.where(at == 1, values[:, 2:3], factor)
        factor_ref[k] = jnp.where(at == 2, values[:, 1:2], factor)
    fill_waves(low_ref[...][None, :].astype(jnp.float32), orders_total, high_ref, rest_ref, 32)


def product_kernel(dims, sent_ref, high_ref, rest_ref, out_ref):
    used, shells, scale = dims
    turned = sent_ref[...].astype(jnp.float32).T[:used].astype(jnp.bfloat16)
    grid = jnp.dot(turned, high_ref[...], preferred_element_type=jnp.float32)
    grid = grid + jnp.dot(turned, rest_ref[...], preferred_element_type=jnp.float32)
    products = grid * pltpu.roll(grid, used - shells, 0)
    high = products.astype(jnp.bfloat16)
    rest = (products - high.astype(jnp.float32)).astype(jnp.bfloat16)
    both = lax.dot_general(
        high_ref[...], jnp.concatenate([high, rest], axis=0), NT, preferred_element_type=jnp.float32
    )
    totals = lax.dot_general(rest_ref[...], high, NT, preferred_element_type=jnp.float32)
    totals = totals + both[:, :used] + both[:, used:]
    answers = (totals * scale).astype(jnp.bfloat16)
    out_ref[...] = jnp.concatenate(
        [answers, jnp.zeros((answers.shape[0], LANES - used), jnp.bfloat16)], axis=1
    )


def analysis_sums(dims, low_ref, sent_ref, table_ref, spread_ref, emit):
    pairs_dev, block, count, mode_count, orders_total = dims
    rows_total = table_ref.shape[1]
    chunk_rows = sent_ref.shape[0] // mode_count
    group = lax.axis_index("mode") * pairs_dev
    spread_ref[...] = sent_ref[...].astype(jnp.float32).reshape(spread_ref.shape)
    lane_block = lax.broadcasted_iota(jnp.int32, (mode_count, LANES), 1) // block
    parts = [jnp.zeros((mode_count, LANES), jnp.float32) for _ in range(count)]
    for row in range(chunk_rows):
        piece = spread_ref[:, row, :]
        for i in range(count):
            moved = pltpu.roll(piece, (block * (row - i)) % LANES, 1)
            parts[i] = jnp.where(lane_block == row, moved, parts[i])
    returned = jnp.concatenate(parts, axis=0).T.astype(jnp.bfloat16)
    per_pair = returned.shape[0] // pairs_dev
    half = block // 2
    for pair in range(pairs_dev):
        lower = own_lower(low_ref, group + pair)
        members, signs = row_factors(lower, (1, rows_total), orders_total)
        sums = lax.dot_general(
            returned[pair * per_pair : (pair + 1) * per_pair],
            table_ref[pair],
            NT,
            preferred_element_type=jnp.float32,
        )
        for part in range(2):
            total = jnp.zeros((half, rows_total), jnp.float32)
            for k in range(2):
                at = (k * 2 + part) * block
                north = sums[at : at + half]
                south = sums[at + half : at + block]
                total = jnp.where(members[k], north + signs[k] * south, total)
            emit(pair, part, lower, total)


def analysis_kernel(dims, low_ref, sent_ref, table_ref, out_ref, spread_ref):
    def emit(pair, part, lower, total):
        out_ref[pair, part] = total

    analysis_sums(dims, low_ref, sent_ref, table_ref, spread_ref, emit)


def step_kernel(
    dims, low_ref, factor_ref, sent_ref, table_ref, state_ref, out_ref, spread_ref
):
    orders_total = dims[-1]
    rows_total = table_ref.shape[1]
    half = dims[1] // 2
    fields = (0, 2, 1, 0)
    at = lax.broadcasted_iota(jnp.int32, (half, 1), 0)
    upper = at % 2 == 1

    def other(value):
        return jnp.where(upper, pltpu.roll(value, 1, 0), pltpu.roll(value, half - 1, 0))

    rate = factor_ref[0, :, 0:1]
    strength = factor_ref[1, :, 0:1]
    radius = inner_radius + (jnp.where(upper, 1.0, 0.0) + 0.5) * shell_step
    inverse = (shell_step * shell_step) / (radius * radius)
    row = lax.broadcasted_iota(jnp.int32, (1, rows_total), 1)
    cache = {}

    def emit(pair, part, lower, total):
        if pair not in cache:
            degree = jnp.where(row < orders_total - lower, lower + row, row - 1).astype(jnp.float32)
            damping = (degree * (degree + 1.0)) * inverse
            diagonal = 1.0 + rate * (2.0 + damping)
            crossed = other(diagonal)
            factor = 1.0 / (diagonal * crossed - rate * rate)
            cache[pair] = (damping, crossed * factor, rate * factor)
        damping, own, across = cache[pair]
        state = state_rows(state_ref, pair, part, fields)
        laplace = other(state) - 2.0 * state - damping * state
        drive = state + rate * (laplace + strength * total)
        updated = own * drive + across * other(drive)
        for k, f in enumerate(fields[:3]):
            for s in range(2):
                out_ref[pair, f, s, part : part + 1, :] = updated[2 * k + s : 2 * k + s + 1]

    analysis_sums(dims, low_ref, sent_ref, table_ref, spread_ref, emit)


def vmem(count):
    return [pl.BlockSpec(memory_space=pltpu.VMEM)] * count


def row_lower(low_ref, first, rows, pairs_dev):
    at = lax.broadcasted_iota(jnp.int32, (rows, 1), 0)
    lower = jnp.zeros((rows, 1), jnp.int32)
    for pair in range(pairs_dev):
        lower = jnp.where(at // (rows // pairs_dev) == pair, own_lower(low_ref, first + pair), lower)
    return at, lower


def row_members(at, lower, rows_total, orders_total):
    row = lax.broadcasted_iota(jnp.int32, (1, rows_total), 1)
    upper = (at // 2) % 2 == 1
    edge = orders_total - lower
    member = jnp.logical_xor(row < edge, upper)
    odd = ((row + jnp.where(upper, edge, 0)) & 1) == 1
    return member, odd


def paired_state(state_ref, field, shell):
    pairs_dev = state_ref.shape[0]
    pieces = [state_ref[pair, field, shell] for pair in range(pairs_dev) for _ in range(2)]
    return jnp.concatenate(pieces, axis=0)


def wave_values(turns, lon_total):
    quad = jnp.floor(turns * (4.0 / lon_total) + 0.5)
    angle = (turns - quad * (lon_total / 4)) * (2.0 * math.pi / lon_total)
    square = angle * angle
    cosine = 1.0 + square * (
        -0.5 + square * (1.0 / 24 + square * (-1.0 / 720 + square * (1.0 / 40320)))
    )
    sine = 1.0 / 120 + square * (-1.0 / 5040 + square * (1.0 / 362880))
    sine = angle * (1.0 + square * (-1.0 / 6 + square * sine))
    quad = quad.astype(jnp.int32)
    swap = (quad & 1) == 1
    cosine, sine = (jnp.where(swap, sine, cosine), jnp.where(swap, cosine, sine))
    cosine = jnp.where(((quad + 1) & 2) == 2, -cosine, cosine)
    sine = jnp.where((quad & 2) == 2, -sine, sine)
    return cosine, sine


def third_factors(order, is_cosine, at):
    third = math.sqrt(0.75)
    turn = at * order
    turn = turn - 3.0 * jnp.floor((turn + 0.5) * (1.0 / 3.0))
    cos_at = jnp.where(turn == 0.0, 1.0, -0.5)
    sin_at = jnp.where(turn == 0.0, 0.0, jnp.where(turn == 1.0, third, -third))
    by_cosine = jnp.where(is_cosine, cos_at, -sin_at)
    by_sine = jnp.where(is_cosine, -sin_at, -cos_at)
    return by_cosine, by_sine


def two_terms(value):
    high = value.astype(jnp.bfloat16)
    return high, (value - high.astype(jnp.float32)).astype(jnp.bfloat16)


def slot_device(slot, mode_count):
    return ((SLOT_STEP * slot) ^ SLOT_FLIP) & (mode_count - 1)


def band_of(device, mode_count):
    return (device & 1) | (((device // (mode_count // 4)) & 1) << 1)


def member_step(mask, mode_count):
    return (mask & 1) | ((mask >> 1) * (mode_count // 4))


def band_synthesis_kernel(
    dims,
    low_ref,
    rate_ref,
    coupling_ref,
    state_ref,
    table_ref,
    out_ref,
    high_ref,
    rest_ref,
    own_ref,
    factor_ref,
):
    group, mode_count, orders_total = dims
    pairs_dev, fields, shells, _, rows_total = state_ref.shape
    rows = out_ref.shape[0] // mode_count
    me = lax.axis_index("mode")
    at, lower = row_lower(low_ref, me * pairs_dev, rows, pairs_dev)
    member, odd = row_members(at, lower, rows_total, orders_total)
    order = jnp.where((at // 2) % 2 == 1, orders_total - 1 - lower, lower)
    weight = jnp.where(order == 0, 1.0, 2.0)
    north = jnp.where(member, weight, 0.0)
    south = jnp.where(odd, -north, north)
    state = [[paired_state(state_ref, f, s) for f in range(fields)] for s in range(shells)]
    fourier = None
    for pair in range(pairs_dev):
        mine = at // (rows // pairs_dev) == pair
        left = [
            state[s][f] * jnp.where(mine, factor, 0.0)
            for factor in (north, south)
            for s in range(shells)
            for f in range(fields)
        ]
        left = jnp.concatenate(left, axis=0).astype(jnp.bfloat16)
        part = jnp.dot(left, table_ref[pair], preferred_element_type=jnp.float32)
        fourier = part if fourier is None else fourier + part
    fourier = fourier.astype(jnp.bfloat16).astype(jnp.float32)
    width = LANES // group
    lane_block = lax.broadcasted_iota(jnp.int32, (fields * rows, LANES), 1) // width
    for band in range(group):
        piece = None
        for block in range(group):
            source = fourier[block * fields * rows : (block + 1) * fields * rows]
            moved = pltpu.roll(source, (width * (block - band)) % LANES, 1)
            piece = moved if piece is None else jnp.where(lane_block == block, moved, piece)
        for field in range(fields):
            value = piece[field * rows : (field + 1) * rows].astype(jnp.bfloat16)
            for slot in range(mode_count):
                if band_of(slot_device(slot, mode_count), mode_count) == band:
                    out_ref[slot * rows : (slot + 1) * rows, field * LANES : (field + 1) * LANES] = value

    lon_total, columns = high_ref.shape
    span = lon_total // 3
    low_row = low_ref[...][None, :].astype(jnp.float32)
    pair_at = lax.broadcasted_iota(jnp.int32, (low_row.shape[1], columns), 0)
    column = lax.broadcasted_iota(jnp.int32, (low_row.shape[1], columns), 1)
    device = slot_device(column // rows, mode_count)
    spread = jnp.where(device * pairs_dev + (column % rows) // 4 == pair_at, 1.0, 0.0).astype(jnp.bfloat16)
    lowers = jnp.broadcast_to(low_row, (8, low_row.shape[1])).astype(jnp.bfloat16)
    lowers = jnp.dot(lowers, spread, preferred_element_type=jnp.float32)[0:1]
    column = lax.broadcasted_iota(jnp.int32, (1, columns), 1)
    orders = jnp.where((column // 2) % 2 == 0, lowers, orders_total - 1 - lowers)
    is_cosine = column % 2 == 0
    factors = [third_factors(orders, is_cosine, third) for third in range(3)]
    step = min(span, 32)
    for base in range(0, span, step):
        lon = (base + lax.broadcasted_iota(jnp.int32, (step, 1), 0)).astype(jnp.float32)
        cosine, sine = wave_values(lon * orders, lon_total)
        for third, (by_cosine, by_sine) in enumerate(factors):
            high, rest = two_terms(cosine * by_cosine + sine * by_sine)
            high_ref[third * span + base : third * span + base + step, :] = high
            rest_ref[third * span + base : third * span + base + step, :] = rest
    count = group * rows
    at = lax.broadcasted_iota(jnp.int32, (count, 1), 0)
    device = me ^ member_step(at // rows, mode_count)
    pair_index = device * pairs_dev + (at % rows) // 4
    pair_lane = lax.broadcasted_iota(jnp.int32, (count, low_row.shape[1]), 1)
    lowers = jnp.sum(jnp.where(pair_lane == pair_index, low_row, 0.0), axis=1, keepdims=True)
    orders = jnp.where((at // 2) % 2 == 0, lowers, orders_total - 1 - lowers)
    is_cosine = at % 2 == 0
    lon = lax.broadcasted_iota(jnp.int32, (1, span), 1).astype(jnp.float32)
    cosine, sine = wave_values(lon * orders, lon_total)
    for third in range(3):
        by_cosine, by_sine = third_factors(orders, is_cosine, third)
        high, rest = two_terms(cosine * by_cosine + sine * by_sine)
        own_ref[:count, third * span : (third + 1) * span] = high
        own_ref[count:, third * span : (third + 1) * span] = rest
    for k, ref in enumerate((rate_ref, coupling_ref)):
        for f in range(fields):
            factor_ref[k, f] = jnp.broadcast_to(ref[...][None, f : f + 1], (8, LANES))


def band_product_kernel(scale, sent_ref, high_ref, rest_ref, own_ref, *out_refs):
    sent = sent_ref[...]
    both = jnp.concatenate([high_ref[...], rest_ref[...]], axis=0)
    grid = jnp.dot(both, sent, preferred_element_type=jnp.float32)
    grid = grid[: high_ref.shape[0]] + grid[high_ref.shape[0] :]
    width = sent.shape[1] // 3
    first, second, third = (grid[:, f * width : (f + 1) * width] for f in range(3))
    products = jnp.concatenate([first * second, first * third, second * third], axis=1)
    high, rest = two_terms(products)
    count = own_ref.shape[0] // 2
    both = jnp.dot(own_ref[...], high, preferred_element_type=jnp.float32)
    totals = jnp.dot(own_ref[:count], rest, preferred_element_type=jnp.float32)
    totals = totals + both[:count] + both[count:]
    answers = (totals * scale).astype(jnp.bfloat16)
    rows = count // len(out_refs)
    for at, out_ref in enumerate(out_refs):
        out_ref[...] = answers[at * rows : (at + 1) * rows]


def band_step_kernel(dims, low_ref, factor_ref, state_ref, table_ref, *refs):
    group, mode_count, orders_total = dims
    sent_refs, out_ref = (refs[:group], refs[group])
    pairs_dev, fields, shells, _, rows_total = state_ref.shape
    rows = sent_refs[0].shape[0]
    me = lax.axis_index("mode")
    at, lower = row_lower(low_ref, me * pairs_dev, rows, pairs_dev)
    member, odd = row_members(at, lower, rows_total, orders_total)
    width = LANES // group
    lane_block = lax.broadcasted_iota(jnp.int32, (fields * rows, LANES), 1) // width
    pieces = []
    for ref in sent_refs:
        value = ref[...].astype(jnp.float32)
        pieces.append(
            jnp.concatenate([value[:, f * LANES : (f + 1) * LANES] for f in range(fields)], axis=0)
        )
    returned = []
    for block in range(group):
        merged = jnp.zeros((fields * rows, LANES), jnp.float32)
        for mask, piece in enumerate(pieces):
            band = band_of(me, mode_count) ^ mask
            moved = pltpu.roll(piece, (width * (band - block + group)) % LANES, 1)
            merged = jnp.where(lane_block == band, moved, merged)
        returned.append(merged)
    returned = jnp.concatenate(returned, axis=0).astype(jnp.bfloat16)
    sums = [
        lax.dot_general(returned, table_ref[pair], NT, preferred_element_type=jnp.float32)
        for pair in range(pairs_dev)
    ]
    row = lax.broadcasted_iota(jnp.int32, (1, rows_total), 1)
    degree = jnp.where(row < orders_total - lower, lower + row, row - 1).astype(jnp.float32)
    degree = degree * (degree + 1.0)
    damping = []
    for s in range(shells):
        radius = inner_radius + (s + 0.5) * shell_step
        damping.append(degree * (shell_step * shell_step / (radius * radius)))
    by_pair = at // (rows // pairs_dev)
    for f in range(fields):
        rate = factor_ref[0, f, :, 0:1]
        strength = factor_ref[1, f, :, 0:1]
        state, drive, diagonal = ([], [], [])
        for s in range(shells):
            state.append(paired_state(state_ref, f, s))
            diagonal.append(1.0 + rate * (2.0 + damping[s]))
        for s in range(shells):
            halves = []
            for h in range(2):
                start = ((h * shells + s) * fields + f) * rows
                value = sums[0][start : start + rows]
                for pair in range(1, pairs_dev):
                    value = jnp.where(by_pair == pair, sums[pair][start : start + rows], value)
                halves.append(value)
            total = halves[0] + jnp.where(odd, -halves[1], halves[1])
            total = jnp.where(member, total, 0.0)
            total = total + pltpu.roll(total, rows - 2, 0)
            laplace = state[1 - s] - 2.0 * state[s] - damping[s] * state[s]
            drive.append(state[s] + rate * (laplace + strength * total))
        factor = 1.0 / (diagonal[0] * diagonal[1] - rate * rate)
        for s in range(shells):
            updated = (diagonal[1 - s] * drive[s] + rate * drive[1 - s]) * factor
            for pair in range(pairs_dev):
                start = pair * (rows // pairs_dev)
                out_ref[pair, f, s] = updated[start : start + 2]


def banded(group, spectral_state, synthesis_table, low_orders, diffusion, coupling):
    pairs_dev, field_count, _, part_count, rows_total = spectral_state.shape
    half_lat = synthesis_table.shape[2]
    orders_total = rows_total - 1
    lon_total = 3 * orders_total
    mode_count = lax.axis_size("mode")
    rows = pairs_dev * 2 * part_count
    columns = rows * mode_count
    scale = 2.0 * math.sqrt(orders_total * rows_total / (2 * half_lat * lon_total))

    def like(shape, dtype=jnp.bfloat16):
        return jax.ShapeDtypeStruct(shape, dtype)

    chunks, wave_high, wave_rest, own_waves, factors = pl.pallas_call(
        functools.partial(band_synthesis_kernel, (group, mode_count, orders_total)),
        out_shape=[
            like((columns, field_count * LANES)),
            like((lon_total, columns)),
            like((lon_total, columns)),
            like((2 * group * rows, lon_total)),
            like((2, field_count, 8, LANES), jnp.float32),
        ],
        in_specs=vmem(5),
        out_specs=vmem(5),
        compiler_params=GRANT,
        name="synthesis",
    )(low_orders, diffusion, coupling, spectral_state, synthesis_table)
    slots = [slot_device(slot, mode_count) for slot in range(mode_count)]
    pieces = lax.all_to_all(
        chunks, "mode", split_axis=0, concat_axis=0, tiled=True, axis_index_groups=[slots]
    )
    answers = pl.pallas_call(
        functools.partial(band_product_kernel, scale),
        out_shape=[like((rows, field_count * LANES))] * group,
        in_specs=vmem(4),
        out_specs=vmem(group),
        compiler_params=GRANT,
        name="products",
    )(pieces, wave_high, wave_rest, own_waves)
    returned = [answers[0]]
    for mask in range(1, group):
        ring = [(i, i ^ member_step(mask, mode_count)) for i in range(mode_count)]
        returned.append(lax.ppermute(answers[mask], "mode", ring))
    return pl.pallas_call(
        functools.partial(band_step_kernel, (group, mode_count, orders_total)),
        out_shape=like(spectral_state.shape, jnp.float32),
        in_specs=vmem(4 + group),
        out_specs=pl.BlockSpec(memory_space=pltpu.VMEM),
        compiler_params=GRANT,
        name="step",
    )(low_orders, factors, spectral_state, synthesis_table, *returned)


def body(spectral_state, synthesis_table, low_orders, diffusion, coupling):
    radial_count = lax.axis_size("radial")
    if radial_count > 1:
        synthesis_table = lax.all_gather(synthesis_table, "radial", axis=2, tiled=True)
    pairs_dev, field_count, shell_count, part_count, rows_total = spectral_state.shape
    half_lat = synthesis_table.shape[2]
    lat_total = 2 * half_lat
    orders_total = rows_total - 1
    lon_total = 3 * orders_total
    mode_count = lax.axis_size("mode")
    chunk_rows = pairs_dev * 2 * part_count
    column_count = chunk_rows * mode_count
    count = half_lat // mode_count
    half = (field_count + 1) * shell_count
    block = 2 * half
    used = count * block
    assert half == 8 and chunk_rows * block == LANES and used <= LANES // 2 and part_count == 2
    scale = 2.0 * math.sqrt(orders_total * rows_total / (lat_total * lon_total))
    group = 2 * shell_count * half_lat // LANES
    if radial_count == 1 and shell_count == 2 and group == 4 and mode_count >= 8 and mode_count & (mode_count - 1) == 0:
        return banded(group, spectral_state, synthesis_table, low_orders, diffusion, coupling)
    spread = pltpu.VMEM((mode_count, chunk_rows, LANES), jnp.float32)
    sent = jax.ShapeDtypeStruct((column_count, LANES), jnp.bfloat16)
    table_shape = jax.ShapeDtypeStruct((column_count, lon_total), jnp.bfloat16)
    factor_shape = jax.ShapeDtypeStruct((2, half, LANES), jnp.float32)
    chunks, wave_high, wave_rest, factors = pl.pallas_call(
        functools.partial(synthesis_kernel, (pairs_dev, block, mode_count, orders_total)),
        out_shape=[sent, table_shape, table_shape, factor_shape],
        in_specs=vmem(5),
        out_specs=vmem(4),
        scratch_shapes=[spread],
        compiler_params=GRANT,
        name="synthesis",
    )(low_orders, diffusion, coupling, spectral_state, synthesis_table)
    pieces = lax.all_to_all(chunks, "mode", split_axis=0, concat_axis=0, tiled=True)
    answers = pl.pallas_call(
        functools.partial(product_kernel, (used, shell_count, scale)),
        out_shape=sent,
        in_specs=vmem(3),
        out_specs=pl.BlockSpec(memory_space=pltpu.VMEM),
        compiler_params=GRANT,
        name="products",
    )(pieces, wave_high, wave_rest)
    returned = lax.all_to_all(answers, "mode", split_axis=0, concat_axis=0, tiled=True)
    dims = (pairs_dev, block, count, mode_count, orders_total)
    if radial_count == 1 and shell_count == 2:
        return pl.pallas_call(
            functools.partial(step_kernel, dims),
            out_shape=jax.ShapeDtypeStruct(spectral_state.shape, jnp.float32),
            in_specs=vmem(5),
            out_specs=pl.BlockSpec(memory_space=pltpu.VMEM),
            scratch_shapes=[spread],
            compiler_params=GRANT,
            name="step",
        )(low_orders, factors, returned, synthesis_table, spectral_state)
    nonlinear = pl.pallas_call(
        functools.partial(analysis_kernel, dims),
        out_shape=jax.ShapeDtypeStruct((pairs_dev, part_count, half, rows_total), jnp.float32),
        in_specs=vmem(3),
        out_specs=pl.BlockSpec(memory_space=pltpu.VMEM),
        scratch_shapes=[spread],
        compiler_params=GRANT,
        name="analysis",
    )(low_orders, returned, synthesis_table)
    nonlinear = nonlinear.reshape(pairs_dev, part_count, field_count + 1, shell_count, rows_total)
    nonlinear = jnp.stack([nonlinear[:, :, 0], nonlinear[:, :, 2], nonlinear[:, :, 1]], axis=1)
    nonlinear = nonlinear.transpose(0, 1, 3, 2, 4)
    return solve(spectral_state, nonlinear, low_orders, diffusion, coupling)


def solve(spectral_state, nonlinear, low_orders, diffusion, coupling):
    pairs_dev, field_count, shell_count, _, rows_total = spectral_state.shape
    orders_total = rows_total - 1
    radial_count = lax.axis_size("radial")
    own = lax.dynamic_slice_in_dim(low_orders, lax.axis_index("mode") * pairs_dev, pairs_dev)
    row_index = lax.iota(jnp.int32, rows_total)[None, :]
    lower_col = own[:, None]
    degree = jnp.where(row_index < orders_total - lower_col, lower_col + row_index, row_index - 1)
    radial_at = lax.axis_index("radial")
    rate_col = diffusion.reshape(1, field_count, 1, 1)
    strength = coupling.reshape(1, field_count, 1, 1)
    degree_term = degree.astype(jnp.float32)
    degree_term = (degree_term * (degree_term + 1.0))[:, None, None, :] * (shell_step * shell_step)
    if radial_count > 1:
        with_edges = with_halo(spectral_state, "radial", 2, 1)
    else:
        with_edges = jnp.pad(spectral_state, ((0, 0), (0, 0), (1, 1), (0, 0), (0, 0)))
    diagonals = []
    drives = []
    for shell_at in range(shell_count):
        radius = (
            inner_radius
            + ((radial_at * shell_count + shell_at).astype(jnp.float32) + 0.5) * shell_step
        )
        damping = degree_term / (radius * radius)
        middle = with_edges[:, :, shell_at + 1]
        laplace = (
            with_edges[:, :, shell_at + 2]
            - 2.0 * middle
            + with_edges[:, :, shell_at]
            - damping * middle
        )
        drives.append(middle + rate_col * (laplace + strength * nonlinear[:, :, shell_at]))
        diagonals.append(1.0 + rate_col * (2.0 + damping))
    narrow_zero = jnp.zeros(diagonals[0].shape, jnp.float32)
    wide_zero = jnp.zeros(drives[0].shape, jnp.float32)
    pivot_prev = narrow_zero
    carry_u, carry_v, carry_w = (wide_zero, narrow_zero, narrow_zero)
    pivots, sweep_u, sweep_v, sweep_w = ([], [], [], [])
    for shell_at in range(shell_count):
        denom_at = diagonals[shell_at] + rate_col * pivot_prev
        pivot_prev = -rate_col / denom_at
        first_drive = rate_col if shell_at == 0 else 0.0
        last_drive = rate_col if shell_at == shell_count - 1 else 0.0
        carry_u = (drives[shell_at] + rate_col * carry_u) / denom_at
        carry_v = (first_drive + rate_col * carry_v) / denom_at
        carry_w = (last_drive + rate_col * carry_w) / denom_at
        pivots.append(pivot_prev)
        sweep_u.append(carry_u)
        sweep_v.append(carry_v)
        sweep_w.append(carry_w)
    solved_u, solved_v, solved_w = ([sweep_u[-1]], [sweep_v[-1]], [sweep_w[-1]])
    for shell_at in range(shell_count - 2, -1, -1):
        solved_u.insert(0, sweep_u[shell_at] - pivots[shell_at] * solved_u[0])
        solved_v.insert(0, sweep_v[shell_at] - pivots[shell_at] * solved_v[0])
        solved_w.insert(0, sweep_w[shell_at] - pivots[shell_at] * solved_w[0])
    if radial_count == 1:
        return jnp.stack(solved_u, axis=2)
    first_u, last_u = (solved_u[0], solved_u[-1])
    first_v, last_v = (solved_v[0], solved_v[-1])
    first_w, last_w = (solved_w[0], solved_w[-1])
    wide_rows = jnp.stack([first_u, last_u])[None]
    narrow_rows = jnp.stack([first_v, first_w, last_v, last_w])[None]
    wide_all, narrow_all = (
        lax.all_gather(wide_rows, "radial", axis=0, tiled=True),
        lax.all_gather(narrow_rows, "radial", axis=0, tiled=True),
    )
    chain_count = lax.axis_size("radial")
    alpha_now, beta_now = (wide_zero, narrow_zero)
    alphas, betas = ([], [])
    for member in range(chain_count):
        alphas.append(alpha_now)
        betas.append(beta_now)
        peer_first_u, peer_last_u = (wide_all[member, 0], wide_all[member, 1])
        peer_first_v, peer_first_w = (narrow_all[member, 0], narrow_all[member, 1])
        peer_last_v, peer_last_w = (narrow_all[member, 2], narrow_all[member, 3])
        shrink = 1.0 - peer_first_v * beta_now
        alpha_new = (
            peer_last_u
            - peer_last_u * peer_first_v * beta_now
            + peer_last_v * alpha_now
            + peer_last_v * peer_first_u * beta_now
        ) / shrink
        beta_new = (
            peer_last_w
            - peer_last_w * peer_first_v * beta_now
            + peer_last_v * peer_first_w * beta_now
        ) / shrink
        alpha_now, beta_now = (alpha_new, beta_new)
    next_first = wide_zero
    firsts = [None] * chain_count
    nexts = [None] * chain_count
    for member in range(chain_count - 1, -1, -1):
        nexts[member] = next_first
        peer_first_u = wide_all[member, 0]
        peer_first_v, peer_first_w = (narrow_all[member, 0], narrow_all[member, 1])
        next_first = (peer_first_u + peer_first_v * alphas[member] + peer_first_w * next_first) / (
            1.0 - peer_first_v * betas[member]
        )
        firsts[member] = next_first
    alpha_prev = lax.dynamic_index_in_dim(jnp.stack(alphas), radial_at, 0, keepdims=False)
    beta_prev = lax.dynamic_index_in_dim(jnp.stack(betas), radial_at, 0, keepdims=False)
    own_first = lax.dynamic_index_in_dim(jnp.stack(firsts), radial_at, 0, keepdims=False)
    next_first = lax.dynamic_index_in_dim(jnp.stack(nexts), radial_at, 0, keepdims=False)
    prev_last = alpha_prev + beta_prev * own_first
    outputs = []
    for shell_at in range(shell_count):
        outputs.append(
            solved_u[shell_at] + prev_last * solved_v[shell_at] + next_first * solved_w[shell_at]
        )
    return jnp.stack(outputs, axis=2)


def solution(mesh):
    placed = (P("mode", None, "radial", None, None), P("mode", None, "radial"), P(), P(), P())
    return jax.shard_map(
        body,
        mesh=mesh,
        in_specs=placed,
        out_specs=P("mode", None, "radial", None, None),
        check_vma=False,
    )
```

```python
import functools
import math

import jax
import jax.numpy as jnp
from jax import lax
from jax.experimental import pallas as pl
from jax.experimental.pallas import tpu as pltpu
from jax.sharding import PartitionSpec as P


inner_radius = 0.538
shell_step = 1.0 / 2048.0
LANES = 128
SLOT_STEP = 11
SLOT_FLIP = 29
GRANT = pltpu.CompilerParams(vmem_limit_bytes=16 * 1024 * 1024)
NT = (((1,), (1,)), ((), ()))


def with_halo(shard, axis, dim, width):
    count, length = (lax.axis_size(axis), shard.shape[dim])
    up = [(i, (i + 1) % count) for i in range(count - 1)]
    down = [(j, i) for i, j in up]
    last = lax.slice_in_dim(shard, length - width, length, axis=dim)
    first = lax.slice_in_dim(shard, 0, width, axis=dim)
    before = lax.ppermute(last, axis, up)
    after = lax.ppermute(first, axis, down)
    return jnp.concatenate([before, shard, after], axis=dim)


def own_lower(low_ref, at):
    low_row = low_ref[...][None, :]
    lane = lax.broadcasted_iota(jnp.int32, low_row.shape, 1)
    return jnp.sum(jnp.where(lane == at, low_row, 0), axis=1, keepdims=True)


def row_factors(lower, shape, orders_total):
    row = lax.broadcasted_iota(jnp.int32, shape, len(shape) - 1)
    in_lower = row < orders_total - lower
    odd_lower = lax.rem(row, 2) == 1
    odd_upper = lax.rem(row + orders_total - lower, 2) == 1
    members = (in_lower, jnp.logical_not(in_lower))
    signs = (jnp.where(odd_lower, -1.0, 1.0), jnp.where(odd_upper, -1.0, 1.0))
    return members, signs


def state_rows(state_ref, pair, part, fields):
    shells = state_ref.shape[2]
    rows = [state_ref[pair, f, s, part : part + 1, :] for f in fields for s in range(shells)]
    return jnp.concatenate(rows, axis=0)


def fill_waves(low_row, orders_total, high_ref, rest_ref, step):
    columns, lon_total = high_ref.shape
    width = lon_total // 3
    lon = lax.broadcasted_iota(jnp.int32, (step, width), 1).astype(jnp.float32)
    pair_lane = lax.broadcasted_iota(jnp.int32, (step, low_row.shape[1]), 1)
    third = math.sqrt(0.75)

    def fill(base):
        column = base + lax.broadcasted_iota(jnp.int32, (step, 1), 0)
        hit = pair_lane == column // 4
        lower = jnp.sum(jnp.where(hit, low_row, 0.0), axis=1, keepdims=True)
        is_lower = (column // 2) % 2 == 0
        is_cosine = column % 2 == 0
        order = jnp.where(is_lower, lower, orders_total - 1 - lower)
        turns = order * lon
        quad = jnp.floor(turns * (4.0 / lon_total) + 0.5)
        angle = (turns - quad * (lon_total / 4)) * (2.0 * math.pi / lon_total)
        square = angle * angle
        cosine = 1.0 + square * (
            -0.5 + square * (1.0 / 24 + square * (-1.0 / 720 + square * (1.0 / 40320)))
        )
        sine = 1.0 / 120 + square * (-1.0 / 5040 + square * (1.0 / 362880))
        sine = angle * (1.0 + square * (-1.0 / 6 + square * sine))
        quad = quad.astype(jnp.int32)
        swap = (quad & 1) == 1
        cosine, sine = (jnp.where(swap, sine, cosine), jnp.where(swap, cosine, sine))
        cosine = jnp.where(((quad + 1) & 2) == 2, -cosine, cosine)
        sine = jnp.where((quad & 2) == 2, -sine, sine)
        for at in range(3):
            turn = at * order
            turn = turn - 3.0 * jnp.floor((turn + 0.5) * (1.0 / 3.0))
            cos_at = jnp.where(turn == 0.0, 1.0, -0.5)
            sin_at = jnp.where(turn == 0.0, 0.0, jnp.where(turn == 1.0, third, -third))
            by_cosine = jnp.where(is_cosine, cos_at, -sin_at)
            by_sine = jnp.where(is_cosine, -sin_at, -cos_at)
            value = cosine * by_cosine + sine * by_sine
            high = value.astype(jnp.bfloat16)
            high_ref[pl.ds(base, step), at * width : (at + 1) * width] = high
            rest_ref[pl.ds(base, step), at * width : (at + 1) * width] = (
                value - high.astype(jnp.float32)
            ).astype(jnp.bfloat16)

    if columns <= 256:
        for base in range(0, columns, step):
            fill(base)
    else:

        @pl.loop(0, columns // step)
        def _(at):
            fill(pl.multiple_of(at * step, step))


def synthesis_kernel(
    dims,
    low_ref,
    rate_ref,
    coupling_ref,
    state_ref,
    table_ref,
    out_ref,
    high_ref,
    rest_ref,
    factor_ref,
    spread_ref,
):
    pairs_dev, block, mode_count, orders_total = dims
    fields = state_ref.shape[1]
    rows_total = state_ref.shape[-1]
    chunk_rows = out_ref.shape[0] // mode_count
    group = lax.axis_index("mode") * pairs_dev
    pieces = []
    for pair in range(pairs_dev):
        lower = own_lower(low_ref, group + pair)
        members, signs = row_factors(lower, (1, rows_total), orders_total)
        coeffs = [state_rows(state_ref, pair, part, (*range(fields), 0)) for part in range(2)]
        left = []
        for k in range(2):
            order = lower if k == 0 else orders_total - 1 - lower
            weight = jnp.where(order == 0, 1.0, 2.0)
            member = jnp.where(members[k], weight, 0.0)
            for part in range(2):
                left.append(coeffs[part] * member)
                left.append(coeffs[part] * (member * signs[k]))
        left = jnp.concatenate(left, axis=0).astype(jnp.bfloat16)
        pieces.append(jnp.dot(left, table_ref[pair], preferred_element_type=jnp.float32))
    fourier = jnp.concatenate(pieces, axis=0).astype(jnp.bfloat16).astype(jnp.float32)
    turned = fourier.T
    lane_block = lax.broadcasted_iota(jnp.int32, (mode_count, LANES), 1) // block
    count = turned.shape[0] // mode_count
    for row in range(chunk_rows):
        merged = jnp.zeros((mode_count, LANES), jnp.float32)
        for i in range(count):
            part = turned[i * mode_count : (i + 1) * mode_count]
            moved = pltpu.roll(part, (block * (i - row)) % LANES, 1)
            merged = jnp.where(lane_block == i, moved, merged)
        spread_ref[:, row, :] = merged
    out_ref[...] = spread_ref[...].reshape(out_ref.shape).astype(jnp.bfloat16)
    rows = factor_ref.shape[1]
    at = lax.broadcasted_iota(jnp.int32, (rows, LANES), 0) // (rows // (fields + 1))
    for k, ref in enumerate((rate_ref, coupling_ref)):
        values = ref[...][None, :]
        factor = jnp.broadcast_to(values[:, 0:1], (rows, LANES))
        factor = jnp.where(at == 1, values[:, 2:3], factor)
        factor_ref[k] = jnp.where(at == 2, values[:, 1:2], factor)
    fill_waves(low_ref[...][None, :].astype(jnp.float32), orders_total, high_ref, rest_ref, 32)


def product_kernel(dims, sent_ref, high_ref, rest_ref, out_ref):
    used, shells, scale = dims
    turned = sent_ref[...].astype(jnp.float32).T[:used].astype(jnp.bfloat16)
    grid = jnp.dot(turned, high_ref[...], preferred_element_type=jnp.float32)
    grid = grid + jnp.dot(turned, rest_ref[...], preferred_element_type=jnp.float32)
    products = grid * pltpu.roll(grid, used - shells, 0)
    high = products.astype(jnp.bfloat16)
    rest = (products - high.astype(jnp.float32)).astype(jnp.bfloat16)
    both = lax.dot_general(
        high_ref[...], jnp.concatenate([high, rest], axis=0), NT, preferred_element_type=jnp.float32
    )
    totals = lax.dot_general(rest_ref[...], high, NT, preferred_element_type=jnp.float32)
    totals = totals + both[:, :used] + both[:, used:]
    answers = (totals * scale).astype(jnp.bfloat16)
    out_ref[...] = jnp.concatenate(
        [answers, jnp.zeros((answers.shape[0], LANES - used), jnp.bfloat16)], axis=1
    )


def analysis_sums(dims, low_ref, sent_ref, table_ref, spread_ref, emit):
    pairs_dev, block, count, mode_count, orders_total = dims
    rows_total = table_ref.shape[1]
    chunk_rows = sent_ref.shape[0] // mode_count
    group = lax.axis_index("mode") * pairs_dev
    spread_ref[...] = sent_ref[...].astype(jnp.float32).reshape(spread_ref.shape)
    lane_block = lax.broadcasted_iota(jnp.int32, (mode_count, LANES), 1) // block
    parts = [jnp.zeros((mode_count, LANES), jnp.float32) for _ in range(count)]
    for row in range(chunk_rows):
        piece = spread_ref[:, row, :]
        for i in range(count):
            moved = pltpu.roll(piece, (block * (row - i)) % LANES, 1)
            parts[i] = jnp.where(lane_block == row, moved, parts[i])
    returned = jnp.concatenate(parts, axis=0).T.astype(jnp.bfloat16)
    per_pair = returned.shape[0] // pairs_dev
    half = block // 2
    for pair in range(pairs_dev):
        lower = own_lower(low_ref, group + pair)
        members, signs = row_factors(lower, (1, rows_total), orders_total)
        sums = lax.dot_general(
            returned[pair * per_pair : (pair + 1) * per_pair],
            table_ref[pair],
            NT,
            preferred_element_type=jnp.float32,
        )
        for part in range(2):
            total = jnp.zeros((half, rows_total), jnp.float32)
            for k in range(2):
                at = (k * 2 + part) * block
                north = sums[at : at + half]
                south = sums[at + half : at + block]
                total = jnp.where(members[k], north + signs[k] * south, total)
            emit(pair, part, lower, total)


def analysis_kernel(dims, low_ref, sent_ref, table_ref, out_ref, spread_ref):
    def emit(pair, part, lower, total):
        out_ref[pair, part] = total

    analysis_sums(dims, low_ref, sent_ref, table_ref, spread_ref, emit)


def step_kernel(
    dims, low_ref, factor_ref, sent_ref, table_ref, state_ref, out_ref, spread_ref
):
    orders_total = dims[-1]
    rows_total = table_ref.shape[1]
    half = dims[1] // 2
    fields = (0, 2, 1, 0)
    at = lax.broadcasted_iota(jnp.int32, (half, 1), 0)
    upper = at % 2 == 1

    def other(value):
        return jnp.where(upper, pltpu.roll(value, 1, 0), pltpu.roll(value, half - 1, 0))

    rate = factor_ref[0, :, 0:1]
    strength = factor_ref[1, :, 0:1]
    radius = inner_radius + (jnp.where(upper, 1.0, 0.0) + 0.5) * shell_step
    inverse = (shell_step * shell_step) / (radius * radius)
    row = lax.broadcasted_iota(jnp.int32, (1, rows_total), 1)
    cache = {}

    def emit(pair, part, lower, total):
        if pair not in cache:
            degree = jnp.where(row < orders_total - lower, lower + row, row - 1).astype(jnp.float32)
            damping = (degree * (degree + 1.0)) * inverse
            diagonal = 1.0 + rate * (2.0 + damping)
            crossed = other(diagonal)
            factor = 1.0 / (diagonal * crossed - rate * rate)
            cache[pair] = (damping, crossed * factor, rate * factor)
        damping, own, across = cache[pair]
        state = state_rows(state_ref, pair, part, fields)
        laplace = other(state) - 2.0 * state - damping * state
        drive = state + rate * (laplace + strength * total)
        updated = own * drive + across * other(drive)
        for k, f in enumerate(fields[:3]):
            for s in range(2):
                out_ref[pair, f, s, part : part + 1, :] = updated[2 * k + s : 2 * k + s + 1]

    analysis_sums(dims, low_ref, sent_ref, table_ref, spread_ref, emit)


def vmem(count):
    return [pl.BlockSpec(memory_space=pltpu.VMEM)] * count


def row_lower(low_ref, first, rows, pairs_dev):
    at = lax.broadcasted_iota(jnp.int32, (rows, 1), 0)
    lower = jnp.zeros((rows, 1), jnp.int32)
    for pair in range(pairs_dev):
        lower = jnp.where(at // (rows // pairs_dev) == pair, own_lower(low_ref, first + pair), lower)
    return at, lower


def row_members(at, lower, rows_total, orders_total):
    row = lax.broadcasted_iota(jnp.int32, (1, rows_total), 1)
    upper = (at // 2) % 2 == 1
    edge = orders_total - lower
    member = jnp.logical_xor(row < edge, upper)
    odd = ((row + jnp.where(upper, edge, 0)) & 1) == 1
    return member, odd


def paired_state(state_ref, field, shell):
    pairs_dev = state_ref.shape[0]
    pieces = [state_ref[pair, field, shell] for pair in range(pairs_dev) for _ in range(2)]
    return jnp.concatenate(pieces, axis=0)


def wave_values(turns, lon_total):
    quad = jnp.floor(turns * (4.0 / lon_total) + 0.5)
    angle = (turns - quad * (lon_total / 4)) * (2.0 * math.pi / lon_total)
    square = angle * angle
    cosine = 1.0 + square * (
        -0.5 + square * (1.0 / 24 + square * (-1.0 / 720 + square * (1.0 / 40320)))
    )
    sine = 1.0 / 120 + square * (-1.0 / 5040 + square * (1.0 / 362880))
    sine = angle * (1.0 + square * (-1.0 / 6 + square * sine))
    quad = quad.astype(jnp.int32)
    swap = (quad & 1) == 1
    cosine, sine = (jnp.where(swap, sine, cosine), jnp.where(swap, cosine, sine))
    cosine = jnp.where(((quad + 1) & 2) == 2, -cosine, cosine)
    sine = jnp.where((quad & 2) == 2, -sine, sine)
    return cosine, sine


def third_factors(order, is_cosine, at):
    third = math.sqrt(0.75)
    turn = at * order
    turn = turn - 3.0 * jnp.floor((turn + 0.5) * (1.0 / 3.0))
    cos_at = jnp.where(turn == 0.0, 1.0, -0.5)
    sin_at = jnp.where(turn == 0.0, 0.0, jnp.where(turn == 1.0, third, -third))
    by_cosine = jnp.where(is_cosine, cos_at, -sin_at)
    by_sine = jnp.where(is_cosine, -sin_at, -cos_at)
    return by_cosine, by_sine


def two_terms(value):
    high = value.astype(jnp.bfloat16)
    return high, (value - high.astype(jnp.float32)).astype(jnp.bfloat16)


def slot_device(slot, mode_count):
    return ((SLOT_STEP * slot) ^ SLOT_FLIP) & (mode_count - 1)


def band_of(device, mode_count):
    return (device & 1) | (((device // (mode_count // 4)) & 1) << 1)


def member_step(mask, mode_count):
    return (mask & 1) | ((mask >> 1) * (mode_count // 4))


def band_synthesis_kernel(
    dims,
    low_ref,
    rate_ref,
    coupling_ref,
    state_ref,
    table_ref,
    out_ref,
    high_ref,
    rest_ref,
    factor_ref,
):
    group, mode_count, orders_total = dims
    pairs_dev, fields, shells, _, rows_total = state_ref.shape
    rows = out_ref.shape[0] // mode_count
    me = lax.axis_index("mode")
    at, lower = row_lower(low_ref, me * pairs_dev, rows, pairs_dev)
    member, odd = row_members(at, lower, rows_total, orders_total)
    order = jnp.where((at // 2) % 2 == 1, orders_total - 1 - lower, lower)
    weight = jnp.where(order == 0, 1.0, 2.0)
    north = jnp.where(member, weight, 0.0)
    south = jnp.where(odd, -north, north)
    state = [[paired_state(state_ref, f, s) for f in range(fields)] for s in range(shells)]
    fourier = None
    for pair in range(pairs_dev):
        mine = at // (rows // pairs_dev) == pair
        left = [
            state[s][f] * jnp.where(mine, factor, 0.0)
            for factor in (north, south)
            for s in range(shells)
            for f in range(fields)
        ]
        left = jnp.concatenate(left, axis=0).astype(jnp.bfloat16)
        part = jnp.dot(left, table_ref[pair], preferred_element_type=jnp.float32)
        fourier = part if fourier is None else fourier + part
    fourier = fourier.astype(jnp.bfloat16).astype(jnp.float32)
    width = LANES // group
    lane_block = lax.broadcasted_iota(jnp.int32, (fields * rows, LANES), 1) // width
    for band in range(group):
        piece = None
        for block in range(group):
            source = fourier[block * fields * rows : (block + 1) * fields * rows]
            moved = pltpu.roll(source, (width * (block - band)) % LANES, 1)
            piece = moved if piece is None else jnp.where(lane_block == block, moved, piece)
        for field in range(fields):
            value = piece[field * rows : (field + 1) * rows].astype(jnp.bfloat16)
            for slot in range(mode_count):
                if band_of(slot_device(slot, mode_count), mode_count) == band:
                    out_ref[slot * rows : (slot + 1) * rows, field * LANES : (field + 1) * LANES] = value

    lon_total, columns = high_ref.shape
    span = lon_total // 3
    low_row = low_ref[...][None, :].astype(jnp.float32)
    pair_at = lax.broadcasted_iota(jnp.int32, (low_row.shape[1], columns), 0)
    column = lax.broadcasted_iota(jnp.int32, (low_row.shape[1], columns), 1)
    device = slot_device(column // rows, mode_count)
    spread = jnp.where(device * pairs_dev + (column % rows) // 4 == pair_at, 1.0, 0.0).astype(jnp.bfloat16)
    lowers = jnp.broadcast_to(low_row, (8, low_row.shape[1])).astype(jnp.bfloat16)
    lowers = jnp.dot(lowers, spread, preferred_element_type=jnp.float32)[0:1]
    column = lax.broadcasted_iota(jnp.int32, (1, columns), 1)
    orders = jnp.where((column // 2) % 2 == 0, lowers, orders_total - 1 - lowers)
    is_cosine = column % 2 == 0
    factors = [third_factors(orders, is_cosine, third) for third in range(3)]
    step = min(span, 8)
    for base in range(0, span, step):
        lon = (base + lax.broadcasted_iota(jnp.int32, (step, 1), 0)).astype(jnp.float32)
        cosine, sine = wave_values(lon * orders, lon_total)
        for third, (by_cosine, by_sine) in enumerate(factors):
            high, rest = two_terms(cosine * by_cosine + sine * by_sine)
            high_ref[third * span + base : third * span + base + step, :] = high
            rest_ref[third * span + base : third * span + base + step, :] = rest
    for k, ref in enumerate((rate_ref, coupling_ref)):
        for f in range(fields):
            factor_ref[k, f] = jnp.broadcast_to(ref[...][None, f : f + 1], (8, LANES))


def band_product_kernel(dims, low_ref, sent_ref, high_ref, rest_ref, *refs):
    scale, pairs_dev, mode_count, orders_total = dims
    out_refs, own_ref = (refs[:-1], refs[-1])
    group = len(out_refs)
    rows = out_refs[0].shape[0]
    me = lax.axis_index("mode")
    lon_total = high_ref.shape[0]
    span = lon_total // 3
    low_row = low_ref[...][None, :].astype(jnp.float32)
    count = group * rows
    at = lax.broadcasted_iota(jnp.int32, (count, 1), 0)
    device = me ^ member_step(at // rows, mode_count)
    pair_index = device * pairs_dev + (at % rows) // 4
    pair_lane = lax.broadcasted_iota(jnp.int32, (count, low_row.shape[1]), 1)
    lowers = jnp.sum(jnp.where(pair_lane == pair_index, low_row, 0.0), axis=1, keepdims=True)
    orders = jnp.where((at // 2) % 2 == 0, lowers, orders_total - 1 - lowers)
    is_cosine = at % 2 == 0
    lon = lax.broadcasted_iota(jnp.int32, (1, span), 1).astype(jnp.float32)
    cosine, sine = wave_values(lon * orders, lon_total)
    for third in range(3):
        by_cosine, by_sine = third_factors(orders, is_cosine, third)
        high, rest = two_terms(cosine * by_cosine + sine * by_sine)
        own_ref[:count, third * span : (third + 1) * span] = high
        own_ref[count:, third * span : (third + 1) * span] = rest
    sent = sent_ref[...]
    grid = jnp.dot(high_ref[...], sent, preferred_element_type=jnp.float32)
    grid = grid + jnp.dot(rest_ref[...], sent, preferred_element_type=jnp.float32)
    width = sent.shape[1] // 3
    first, second, third = (grid[:, f * width : (f + 1) * width] for f in range(3))
    products = jnp.concatenate([first * second, first * third, second * third], axis=1)
    high, rest = two_terms(products)
    count = own_ref.shape[0] // 2
    both = jnp.dot(own_ref[...], high, preferred_element_type=jnp.float32)
    totals = jnp.dot(own_ref[:count], rest, preferred_element_type=jnp.float32)
    totals = totals + both[:count] + both[count:]
    answers = (totals * scale).astype(jnp.bfloat16)
    rows = count // len(out_refs)
    for at, out_ref in enumerate(out_refs):
        out_ref[...] = answers[at * rows : (at + 1) * rows]


def band_step_kernel(dims, low_ref, factor_ref, state_ref, table_ref, *refs):
    group, mode_count, orders_total = dims
    sent_refs, out_ref = (refs[:group], refs[group])
    pairs_dev, fields, shells, _, rows_total = state_ref.shape
    rows = sent_refs[0].shape[0]
    me = lax.axis_index("mode")
    at, lower = row_lower(low_ref, me * pairs_dev, rows, pairs_dev)
    member, odd = row_members(at, lower, rows_total, orders_total)
    width = LANES // group
    lane_block = lax.broadcasted_iota(jnp.int32, (fields * rows, LANES), 1) // width
    pieces = []
    for ref in sent_refs:
        value = ref[...].astype(jnp.float32)
        pieces.append(
            jnp.concatenate([value[:, f * LANES : (f + 1) * LANES] for f in range(fields)], axis=0)
        )
    returned = []
    for block in range(group):
        merged = jnp.zeros((fields * rows, LANES), jnp.float32)
        for mask, piece in enumerate(pieces):
            band = band_of(me, mode_count) ^ mask
            moved = pltpu.roll(piece, (width * (band - block + group)) % LANES, 1)
            merged = jnp.where(lane_block == band, moved, merged)
        returned.append(merged)
    returned = jnp.concatenate(returned, axis=0).astype(jnp.bfloat16)
    sums = [
        lax.dot_general(returned, table_ref[pair], NT, preferred_element_type=jnp.float32)
        for pair in range(pairs_dev)
    ]
    row = lax.broadcasted_iota(jnp.int32, (1, rows_total), 1)
    degree = jnp.where(row < orders_total - lower, lower + row, row - 1).astype(jnp.float32)
    degree = degree * (degree + 1.0)
    damping = []
    for s in range(shells):
        radius = inner_radius + (s + 0.5) * shell_step
        damping.append(degree * (shell_step * shell_step / (radius * radius)))
    by_pair = at // (rows // pairs_dev)
    for f in range(fields):
        rate = factor_ref[0, f, :, 0:1]
        strength = factor_ref[1, f, :, 0:1]
        state, drive, diagonal = ([], [], [])
        for s in range(shells):
            state.append(paired_state(state_ref, f, s))
            diagonal.append(1.0 + rate * (2.0 + damping[s]))
        for s in range(shells):
            halves = []
            for h in range(2):
                start = ((h * shells + s) * fields + f) * rows
                value = sums[0][start : start + rows]
                for pair in range(1, pairs_dev):
                    value = jnp.where(by_pair == pair, sums[pair][start : start + rows], value)
                halves.append(value)
            total = halves[0] + jnp.where(odd, -halves[1], halves[1])
            total = jnp.where(member, total, 0.0)
            total = total + pltpu.roll(total, rows - 2, 0)
            laplace = state[1 - s] - 2.0 * state[s] - damping[s] * state[s]
            drive.append(state[s] + rate * (laplace + strength * total))
        factor = 1.0 / (diagonal[0] * diagonal[1] - rate * rate)
        for s in range(shells):
            updated = (diagonal[1 - s] * drive[s] + rate * drive[1 - s]) * factor
            for pair in range(pairs_dev):
                start = pair * (rows // pairs_dev)
                out_ref[pair, f, s] = updated[start : start + 2]


def banded(group, spectral_state, synthesis_table, low_orders, diffusion, coupling):
    pairs_dev, field_count, _, part_count, rows_total = spectral_state.shape
    half_lat = synthesis_table.shape[2]
    orders_total = rows_total - 1
    lon_total = 3 * orders_total
    mode_count = lax.axis_size("mode")
    rows = pairs_dev * 2 * part_count
    columns = rows * mode_count
    scale = 2.0 * math.sqrt(orders_total * rows_total / (2 * half_lat * lon_total))

    def like(shape, dtype=jnp.bfloat16):
        return jax.ShapeDtypeStruct(shape, dtype)

    chunks, wave_high, wave_rest, factors = pl.pallas_call(
        functools.partial(band_synthesis_kernel, (group, mode_count, orders_total)),
        out_shape=[
            like((columns, field_count * LANES)),
            like((lon_total, columns)),
            like((lon_total, columns)),
            like((2, field_count, 8, LANES), jnp.float32),
        ],
        in_specs=vmem(5),
        out_specs=vmem(4),
        compiler_params=GRANT,
        name="synthesis",
    )(low_orders, diffusion, coupling, spectral_state, synthesis_table)
    slots = [slot_device(slot, mode_count) for slot in range(mode_count)]
    pieces = lax.all_to_all(
        chunks, "mode", split_axis=0, concat_axis=0, tiled=True, axis_index_groups=[slots]
    )
    answers = pl.pallas_call(
        functools.partial(band_product_kernel, (scale, pairs_dev, mode_count, orders_total)),
        out_shape=[like((rows, field_count * LANES))] * group,
        in_specs=vmem(4),
        out_specs=vmem(group),
        scratch_shapes=[pltpu.VMEM((2 * group * rows, lon_total), jnp.bfloat16)],
        compiler_params=GRANT,
        name="products",
    )(low_orders, pieces, wave_high, wave_rest)
    returned = [answers[0]]
    for mask in range(1, group):
        ring = [(i, i ^ member_step(mask, mode_count)) for i in range(mode_count)]
        returned.append(lax.ppermute(answers[mask], "mode", ring))
    return pl.pallas_call(
        functools.partial(band_step_kernel, (group, mode_count, orders_total)),
        out_shape=like(spectral_state.shape, jnp.float32),
        in_specs=vmem(4 + group),
        out_specs=pl.BlockSpec(memory_space=pltpu.VMEM),
        compiler_params=GRANT,
        name="step",
    )(low_orders, factors, spectral_state, synthesis_table, *returned)


def body(spectral_state, synthesis_table, low_orders, diffusion, coupling):
    radial_count = lax.axis_size("radial")
    if radial_count > 1:
        synthesis_table = lax.all_gather(synthesis_table, "radial", axis=2, tiled=True)
    pairs_dev, field_count, shell_count, part_count, rows_total = spectral_state.shape
    half_lat = synthesis_table.shape[2]
    lat_total = 2 * half_lat
    orders_total = rows_total - 1
    lon_total = 3 * orders_total
    mode_count = lax.axis_size("mode")
    chunk_rows = pairs_dev * 2 * part_count
    column_count = chunk_rows * mode_count
    count = half_lat // mode_count
    half = (field_count + 1) * shell_count
    block = 2 * half
    used = count * block
    assert half == 8 and chunk_rows * block == LANES and used <= LANES // 2 and part_count == 2
    scale = 2.0 * math.sqrt(orders_total * rows_total / (lat_total * lon_total))
    group = 2 * shell_count * half_lat // LANES
    if radial_count == 1 and shell_count == 2 and group == 4 and mode_count >= 8 and mode_count & (mode_count - 1) == 0:
        return banded(group, spectral_state, synthesis_table, low_orders, diffusion, coupling)
    spread = pltpu.VMEM((mode_count, chunk_rows, LANES), jnp.float32)
    sent = jax.ShapeDtypeStruct((column_count, LANES), jnp.bfloat16)
    table_shape = jax.ShapeDtypeStruct((column_count, lon_total), jnp.bfloat16)
    factor_shape = jax.ShapeDtypeStruct((2, half, LANES), jnp.float32)
    chunks, wave_high, wave_rest, factors = pl.pallas_call(
        functools.partial(synthesis_kernel, (pairs_dev, block, mode_count, orders_total)),
        out_shape=[sent, table_shape, table_shape, factor_shape],
        in_specs=vmem(5),
        out_specs=vmem(4),
        scratch_shapes=[spread],
        compiler_params=GRANT,
        name="synthesis",
    )(low_orders, diffusion, coupling, spectral_state, synthesis_table)
    pieces = lax.all_to_all(chunks, "mode", split_axis=0, concat_axis=0, tiled=True)
    answers = pl.pallas_call(
        functools.partial(product_kernel, (used, shell_count, scale)),
        out_shape=sent,
        in_specs=vmem(3),
        out_specs=pl.BlockSpec(memory_space=pltpu.VMEM),
        compiler_params=GRANT,
        name="products",
    )(pieces, wave_high, wave_rest)
    returned = lax.all_to_all(answers, "mode", split_axis=0, concat_axis=0, tiled=True)
    dims = (pairs_dev, block, count, mode_count, orders_total)
    if radial_count == 1 and shell_count == 2:
        return pl.pallas_call(
            functools.partial(step_kernel, dims),
            out_shape=jax.ShapeDtypeStruct(spectral_state.shape, jnp.float32),
            in_specs=vmem(5),
            out_specs=pl.BlockSpec(memory_space=pltpu.VMEM),
            scratch_shapes=[spread],
            compiler_params=GRANT,
            name="step",
        )(low_orders, factors, returned, synthesis_table, spectral_state)
    nonlinear = pl.pallas_call(
        functools.partial(analysis_kernel, dims),
        out_shape=jax.ShapeDtypeStruct((pairs_dev, part_count, half, rows_total), jnp.float32),
        in_specs=vmem(3),
        out_specs=pl.BlockSpec(memory_space=pltpu.VMEM),
        scratch_shapes=[spread],
        compiler_params=GRANT,
        name="analysis",
    )(low_orders, returned, synthesis_table)
    nonlinear = nonlinear.reshape(pairs_dev, part_count, field_count + 1, shell_count, rows_total)
    nonlinear = jnp.stack([nonlinear[:, :, 0], nonlinear[:, :, 2], nonlinear[:, :, 1]], axis=1)
    nonlinear = nonlinear.transpose(0, 1, 3, 2, 4)
    return solve(spectral_state, nonlinear, low_orders, diffusion, coupling)


def solve(spectral_state, nonlinear, low_orders, diffusion, coupling):
    pairs_dev, field_count, shell_count, _, rows_total = spectral_state.shape
    orders_total = rows_total - 1
    radial_count = lax.axis_size("radial")
    own = lax.dynamic_slice_in_dim(low_orders, lax.axis_index("mode") * pairs_dev, pairs_dev)
    row_index = lax.iota(jnp.int32, rows_total)[None, :]
    lower_col = own[:, None]
    degree = jnp.where(row_index < orders_total - lower_col, lower_col + row_index, row_index - 1)
    radial_at = lax.axis_index("radial")
    rate_col = diffusion.reshape(1, field_count, 1, 1)
    strength = coupling.reshape(1, field_count, 1, 1)
    degree_term = degree.astype(jnp.float32)
    degree_term = (degree_term * (degree_term + 1.0))[:, None, None, :] * (shell_step * shell_step)
    if radial_count > 1:
        with_edges = with_halo(spectral_state, "radial", 2, 1)
    else:
        with_edges = jnp.pad(spectral_state, ((0, 0), (0, 0), (1, 1), (0, 0), (0, 0)))
    diagonals = []
    drives = []
    for shell_at in range(shell_count):
        radius = (
            inner_radius
            + ((radial_at * shell_count + shell_at).astype(jnp.float32) + 0.5) * shell_step
        )
        damping = degree_term / (radius * radius)
        middle = with_edges[:, :, shell_at + 1]
        laplace = (
            with_edges[:, :, shell_at + 2]
            - 2.0 * middle
            + with_edges[:, :, shell_at]
            - damping * middle
        )
        drives.append(middle + rate_col * (laplace + strength * nonlinear[:, :, shell_at]))
        diagonals.append(1.0 + rate_col * (2.0 + damping))
    narrow_zero = jnp.zeros(diagonals[0].shape, jnp.float32)
    wide_zero = jnp.zeros(drives[0].shape, jnp.float32)
    pivot_prev = narrow_zero
    carry_u, carry_v, carry_w = (wide_zero, narrow_zero, narrow_zero)
    pivots, sweep_u, sweep_v, sweep_w = ([], [], [], [])
    for shell_at in range(shell_count):
        denom_at = diagonals[shell_at] + rate_col * pivot_prev
        pivot_prev = -rate_col / denom_at
        first_drive = rate_col if shell_at == 0 else 0.0
        last_drive = rate_col if shell_at == shell_count - 1 else 0.0
        carry_u = (drives[shell_at] + rate_col * carry_u) / denom_at
        carry_v = (first_drive + rate_col * carry_v) / denom_at
        carry_w = (last_drive + rate_col * carry_w) / denom_at
        pivots.append(pivot_prev)
        sweep_u.append(carry_u)
        sweep_v.append(carry_v)
        sweep_w.append(carry_w)
    solved_u, solved_v, solved_w = ([sweep_u[-1]], [sweep_v[-1]], [sweep_w[-1]])
    for shell_at in range(shell_count - 2, -1, -1):
        solved_u.insert(0, sweep_u[shell_at] - pivots[shell_at] * solved_u[0])
        solved_v.insert(0, sweep_v[shell_at] - pivots[shell_at] * solved_v[0])
        solved_w.insert(0, sweep_w[shell_at] - pivots[shell_at] * solved_w[0])
    if radial_count == 1:
        return jnp.stack(solved_u, axis=2)
    first_u, last_u = (solved_u[0], solved_u[-1])
    first_v, last_v = (solved_v[0], solved_v[-1])
    first_w, last_w = (solved_w[0], solved_w[-1])
    wide_rows = jnp.stack([first_u, last_u])[None]
    narrow_rows = jnp.stack([first_v, first_w, last_v, last_w])[None]
    wide_all, narrow_all = (
        lax.all_gather(wide_rows, "radial", axis=0, tiled=True),
        lax.all_gather(narrow_rows, "radial", axis=0, tiled=True),
    )
    chain_count = lax.axis_size("radial")
    alpha_now, beta_now = (wide_zero, narrow_zero)
    alphas, betas = ([], [])
    for member in range(chain_count):
        alphas.append(alpha_now)
        betas.append(beta_now)
        peer_first_u, peer_last_u = (wide_all[member, 0], wide_all[member, 1])
        peer_first_v, peer_first_w = (narrow_all[member, 0], narrow_all[member, 1])
        peer_last_v, peer_last_w = (narrow_all[member, 2], narrow_all[member, 3])
        shrink = 1.0 - peer_first_v * beta_now
        alpha_new = (
            peer_last_u
            - peer_last_u * peer_first_v * beta_now
            + peer_last_v * alpha_now
            + peer_last_v * peer_first_u * beta_now
        ) / shrink
        beta_new = (
            peer_last_w
            - peer_last_w * peer_first_v * beta_now
            + peer_last_v * peer_first_w * beta_now
        ) / shrink
        alpha_now, beta_now = (alpha_new, beta_new)
    next_first = wide_zero
    firsts = [None] * chain_count
    nexts = [None] * chain_count
    for member in range(chain_count - 1, -1, -1):
        nexts[member] = next_first
        peer_first_u = wide_all[member, 0]
        peer_first_v, peer_first_w = (narrow_all[member, 0], narrow_all[member, 1])
        next_first = (peer_first_u + peer_first_v * alphas[member] + peer_first_w * next_first) / (
            1.0 - peer_first_v * betas[member]
        )
        firsts[member] = next_first
    alpha_prev = lax.dynamic_index_in_dim(jnp.stack(alphas), radial_at, 0, keepdims=False)
    beta_prev = lax.dynamic_index_in_dim(jnp.stack(betas), radial_at, 0, keepdims=False)
    own_first = lax.dynamic_index_in_dim(jnp.stack(firsts), radial_at, 0, keepdims=False)
    next_first = lax.dynamic_index_in_dim(jnp.stack(nexts), radial_at, 0, keepdims=False)
    prev_last = alpha_prev + beta_prev * own_first
    outputs = []
    for shell_at in range(shell_count):
        outputs.append(
            solved_u[shell_at] + prev_last * solved_v[shell_at] + next_first * solved_w[shell_at]
        )
    return jnp.stack(outputs, axis=2)


def solution(mesh):
    placed = (P("mode", None, "radial", None, None), P("mode", None, "radial"), P(), P(), P())
    return jax.shard_map(
        body,
        mesh=mesh,
        in_specs=placed,
        out_specs=P("mode", None, "radial", None, None),
        check_vma=False,
    )
```
